256 devices in a mesh: seq: 32 (over z, x_hi, core), fsdp: 8 (over y, x_lo).
Axes of the slice: x: 4 (x_hi: 2, x_lo: 2; x = x_hi * 2 + x_lo), y: 4, z: 8, core: 2. Of those that a mesh axis runs over, the one named last changes fastest.
Arguments:
- queries: bfloat16 [8, 4096, 2048], P('fsdp', 'seq'), may hold values from -6 to 6
- key_vectors: bfloat16 [8, 4096, 2048], P('fsdp', 'seq'), may hold values from -6 to 6
- value_vectors: bfloat16 [8, 4096, 2048], P('fsdp', 'seq'), may hold values from -6 to 6
- out_grad: bfloat16 [8, 4096, 2048], P('fsdp', 'seq'), may hold values from -6 to 6
- out_weight: bfloat16 [2048, 2048], P(None, 'fsdp'), may hold values from -0.125 to 0.125
Outputs:
- query_grad: bfloat16 [8, 4096, 2048], P('fsdp', 'seq')
- key_grad: bfloat16 [8, 4096, 2048], P('fsdp', 'seq')
- value_grad: bfloat16 [8, 4096, 2048], P('fsdp', 'seq')
- weight_grad: float32 [2048, 2048], P('seq', 'fsdp')
The draws below stay inside these ranges and needn't reach their ends.
All inputs are finite; a program needn't handle non-finite values.
Results may differ from the reference program's by a relative error of at most 0.005.
Values may be sent and summed in bfloat16 or wider, within the bound.
A program may use at most 192 MiB of HBM per device.

```python
import math
import jax
import jax.numpy as jnp
from jax import lax

D = 2048
HEADS = 16
HEAD_DIM = 128
BLOCK = 128
HD = 2048
LENGTH = 4096
SEQS = 8


def spiked(values, key, source, target, blocks, factor):
    def block_of(position):
        return (jnp.arange(values.shape[position]) // (values.shape[position] // blocks)).reshape((-1,) + (1,) * (values.ndim - 1 - position))

    near = jax.random.permutation(key, blocks)[block_of(target)]
    second = (block_of(target) + blocks // 2) % blocks
    return jnp.where((block_of(source) == near) | (block_of(source) == second), factor * values, values)


def shard_levels(stream_key, extent, shards, smallest, largest):
    def one(axis_at, parts):
        heights = jax.random.uniform(jax.random.fold_in(jax.random.fold_in(stream_key, 6), axis_at), (parts,), jnp.float32, smallest / len(shards), largest / len(shards))
        return jnp.repeat(jnp.exp(heights), extent[axis_at] // parts).reshape((-1,) + (1,) * (len(extent) - axis_at - 1))

    level = one(*shards[0])
    for cut in shards[1:]:
        level = level * one(*cut)
    return level


def centred(rng, shape, deviation, bound, cuts=(), dtype=jnp.bfloat16):
    array = jax.random.normal(rng, shape, jnp.float32) * deviation
    if len(cuts) > 0:
        array = shard_levels(rng, shape, cuts, -0.22, 0.18) * array
    return jnp.clip(array, min=-bound, max=bound).astype(dtype)


def bell_draw_with(stream_key, dims, deviation, bound, cuts, heavy, dtype=jnp.bfloat16):
    values = deviation * jax.random.normal(stream_key, dims, jnp.float32)
    if cuts:
        values = values * shard_levels(stream_key, dims, cuts, -0.22, 0.18)
    return jnp.clip(spiked(values, jax.random.fold_in(stream_key, 3), *heavy), -bound, bound).astype(dtype)


def setup_inputs(seed: int = 0) -> dict:
    keys = jax.random.split(jax.random.key(seed), 6)
    return {
        "queries": centred(keys[0], (SEQS, LENGTH, HD), 1.0, 6.0, ((0, 8), (1, 32))),
        "key_vectors": centred(keys[1], (SEQS, LENGTH, HD), 1.0, 6.0, ((0, 8), (1, 32))),
        "value_vectors": centred(keys[2], (SEQS, LENGTH, HD), 1.0, 6.0, ((0, 8), (1, 32))),
        "out_grad": bell_draw_with(keys[3], (SEQS, LENGTH, D), 1.0, 6.0, ((0, 8), (1, 32)), (1, 2, 32, 2.75)),
        "out_weight": centred(keys[4], (D, HD), HD ** -0.5, 0.125, ((1, 8),)),
    }


def to_low(values_in):
    return lax.optimization_barrier(values_in.astype(jnp.bfloat16)).astype(jnp.float32)

def block_terms(queries, key_vectors, value_vectors, grads, factor):
    length = queries.shape[0]
    blocks = length // BLOCK
    shape_four = (blocks, BLOCK, HEADS, HEAD_DIM)
    query_wide = queries.reshape(shape_four)
    keys_wide = key_vectors.reshape(shape_four)
    values_wide = value_vectors.reshape(shape_four)
    grads_wide = grads.reshape(shape_four)
    highest = lax.Precision.HIGHEST
    key_value = jnp.einsum('nshd,nshe->nhde', keys_wide, values_wide, precision=highest)
    query_cot = jnp.einsum('nthd,nthe->nhde', query_wide, grads_wide, precision=highest)
    s_before = jnp.cumsum(key_value, 0) - key_value
    g_after = lax.optimization_barrier(jnp.sum(query_cot, 0)) - jnp.cumsum(query_cot, 0)
    causal = jnp.tril(jnp.ones((BLOCK, BLOCK), jnp.float32))
    scores = jnp.einsum('nthd,nshd->nhts', query_wide, keys_wide, precision=highest) * causal
    mixing = jnp.einsum('nthe,nshe->nhts', grads_wide, values_wide, precision=highest) * causal
    scores = to_low(scores)
    mixing = to_low(mixing)
    attended = jnp.einsum('nthd,nhde->nthe', query_wide, s_before, precision=highest)
    attended = attended + jnp.einsum('nhts,nshe->nthe', scores, values_wide, precision=highest)
    query_grad = jnp.einsum('nthe,nhde->nthd', grads_wide, s_before, precision=highest)
    query_grad = query_grad + jnp.einsum('nhts,nshd->nthd', mixing, keys_wide, precision=highest)
    key_grad = jnp.einsum('nshe,nhde->nshd', values_wide, g_after, precision=highest)
    key_grad = key_grad + jnp.einsum('nhts,nthd->nshd', mixing, query_wide, precision=highest)
    value_grad = jnp.einsum('nshd,nhde->nshe', keys_wide, g_after, precision=highest)
    value_grad = value_grad + jnp.einsum('nhts,nthe->nshe', scores, grads_wide, precision=highest)
    flat = (length, HEADS * HEAD_DIM)
    return (factor * attended.reshape(flat), factor * query_grad.reshape(flat), factor * key_grad.reshape(flat), factor * value_grad.reshape(flat))

def reference(queries, key_vectors, value_vectors, out_grad, out_weight):
    seq_count, length, all_width = queries.shape
    grad_rows = out_grad.reshape(seq_count * length, D)
    grad_attn = jnp.dot(grad_rows, out_weight, preferred_element_type=jnp.float32)
    grad_attn = grad_attn.astype(jnp.bfloat16).reshape(seq_count, length, all_width)
    factor = 1.0 / math.sqrt(HEAD_DIM * length)

    def one_sequence(items):
        attended, query_grad, key_grad, value_grad = block_terms(items[0].astype(jnp.float32), items[1].astype(jnp.float32), items[2].astype(jnp.float32), items[3].astype(jnp.float32), factor)
        return (attended.astype(jnp.bfloat16), query_grad.astype(jnp.bfloat16), key_grad.astype(jnp.bfloat16), value_grad.astype(jnp.bfloat16))
    results = lax.map(one_sequence, (queries, key_vectors, value_vectors, grad_attn))
    attended = results[0].reshape(seq_count * length, all_width)
    weight_grad = lax.dot_general(grad_rows, attended, (((0,), (0,)), ((), ())), preferred_element_type=jnp.float32)
    weight_grad = weight_grad * (1.0 / math.sqrt(seq_count * length))
    return (results[1], results[2], results[3], weight_grad)
```

```python
import functools
import math

import jax
import jax.numpy as jnp
from jax import lax
from jax.experimental import pallas as pl
from jax.experimental.pallas import tpu as pltpu
from jax.sharding import PartitionSpec as P

HEADS = 16
HEAD_DIM = 128
BLOCK = 128
MESH = pl.DeviceIdType.MESH
F32 = jnp.float32
BF16 = jnp.bfloat16
NT = (((1,), (1,)), ((), ()))
TN = (((0,), (0,)), ((), ()))


def dot(a, b, dims=(((1,), (0,)), ((), ()))):
    return lax.dot_general(a, b, dims, preferred_element_type=F32)


def head_cols(h):
    return pl.ds(pl.multiple_of(h * HEAD_DIM, HEAD_DIM), HEAD_DIM)


def kernel(
    chips,
    ring,
    factor,
    grad_factor,
    q_ref,
    k_ref,
    v_ref,
    og_ref,
    w_ref,
    qg_ref,
    kg_ref,
    vg_ref,
    wg_ref,
    og_all,
    gbuf,
    gsend,
    att_all,
    att_send,
    contrib,
    xc_send,
    xc_recv,
    a_send,
    a_recv,
    r_send,
    r_recv,
    p_out,
    state,
    acc_a,
    acc_k,
    acc_v,
    part,
    wx_send,
    wx_recv,
    wa_send,
    wa_recv,
    ag_ss,
    ag_rs,
    g_ss,
    g_rs,
    at_ss,
    at_rs,
    x_ss,
    x_rs,
    a_ss,
    a_rs,
):
    s = lax.axis_index("seq")
    f = lax.axis_index("fsdp")
    group = 2 * ring
    half = HEADS // 2
    chip, core = s // 2, s % 2
    mate = s + 1 - 2 * core
    yy, xl = f // 2, f % 2
    xp = f + 1 - 2 * xl
    up = ((yy + 1) % ring) * 2
    down = ((yy + ring - 1) % ring) * 2
    far = ((yy + 2) % ring) * 2
    ol = 1 - xl
    slice_rows = half * HEAD_DIM // chips

    def remote(src, dst, ssem, rsem, dev):
        return pltpu.make_async_remote_copy(
            src_ref=src,
            dst_ref=dst,
            send_sem=ssem,
            recv_sem=rsem,
            device_id=dev,
            device_id_type=MESH,
        )

    barrier = pltpu.get_barrier_semaphore()

    @pl.loop(1, group)
    def _(j):
        pl.semaphore_signal(barrier, inc=1, device_id=(s, (f + j) % group), device_id_type=MESH)

    @pl.loop(1, chips)
    def _(j):
        other = ((chip + j) % chips) * 2 + core
        pl.semaphore_signal(barrier, inc=1, device_id=(other, f), device_id_type=MESH)

    pl.semaphore_signal(barrier, inc=1, device_id=(mate, f), device_id_type=MESH)
    pl.semaphore_wait(barrier, group - 1 + chips - 1 + 1)

    def ag_full(n, slot, dev):
        return remote(og_all.at[slot], og_all.at[slot], ag_ss.at[n], ag_rs.at[slot, 0], (s, dev))

    def ag_own(n, dev):
        return remote(og_ref, og_all.at[f], ag_ss.at[n], ag_rs.at[f, 0], (s, dev))

    def ag_half(n, slot, part_at, dev):
        rows = pl.ds(part_at * (BLOCK // 2), BLOCK // 2)
        view = og_all.at[slot, rows]
        return remote(view, view, ag_ss.at[n], ag_rs.at[slot, part_at], (s, dev))

    ag_own(0, up + xl).start()
    ag_own(1, down + xl).start()
    ag_own(2, xp).start()

    def contrib_rows(b, left, right, first):
        @pl.loop(0, half // 2)
        def _(i):
            for u in range(2):
                h = first + 2 * i + u
                contrib[b, 2 * i + u] = dot(left(h), right(h), TN)

    def pair_start(b, left, right):
        other = (1 - core) * half

        @pl.loop(0, half // 2)
        def _(i):
            for u in range(2):
                h = other + 2 * i + u
                xc_send[b, 2 * i + u] = dot(left(h), right(h), TN).astype(BF16)

        remote(xc_send.at[b], xc_recv.at[b], x_ss.at[2 * b], x_rs.at[2 * b], (mate, f)).start()
        contrib_rows(b, left, right, core * half)

    def a2a_copy(src, dst, n, there):
        return remote(
            src, dst, a_ss.at[n, there], a_rs.at[n, chip], (there * 2 + core, f)
        )

    def a2a_start(src, dst, n):
        @pl.loop(1, chips)
        def _(j):
            there = (chip + j) % chips
            a2a_copy(src.at[there], dst.at[chip], n, there).start()

    def a2a_wait(src, dst, n):
        @pl.loop(1, chips)
        def _(j):
            there = (chip + j) % chips
            remote(
                src.at[there], dst.at[there], a_ss.at[n, there], a_rs.at[n, there],
                (there * 2 + core, f),
            ).wait_recv()

    def a2a_drain(src, dst, n):
        @pl.loop(1, chips)
        def _(j):
            there = (chip + j) % chips
            a2a_copy(src.at[there], dst.at[chip], n, there).wait_send()

    def sum_start(b):
        remote(xc_send.at[b], xc_recv.at[b], x_ss.at[2 * b], x_rs.at[2 * b], (mate, f)).wait_recv()

        @pl.loop(0, chips)
        def _(j):
            head, row = j * slice_rows // HEAD_DIM, pl.multiple_of((j * slice_rows) % HEAD_DIM, slice_rows)
            rows = pl.ds(row, slice_rows)
            total = contrib[b, head, rows] + xc_recv[b, head, rows].astype(F32)
            a_send[b, j] = total.astype(BF16)

        a_recv[b, chip] = a_send[b, chip]
        a2a_start(a_send.at[b], a_recv.at[b], 2 * b)

    def run_start(b, reverse):
        a2a_wait(a_send.at[b], a_recv.at[b], 2 * b)
        total = jnp.zeros((slice_rows, HEAD_DIM), F32)
        for j in range(chips):
            at = chips - 1 - j if reverse else j
            r_send[b, at] = total.astype(BF16)
            total = total + a_recv[b, at].astype(F32)
        r_recv[b, chip] = r_send[b, chip]
        a2a_start(r_send.at[b], r_recv.at[b], 2 * b + 1)

    def state_start(b, reverse):
        a2a_wait(r_send.at[b], r_recv.at[b], 2 * b + 1)
        first = core == (1 if reverse else 0)

        @pl.loop(0, chips)
        def _(j):
            head, row = j * slice_rows // HEAD_DIM, pl.multiple_of((j * slice_rows) % HEAD_DIM, slice_rows)
            rows = pl.ds(row, slice_rows)
            carried = r_recv[b, j].astype(F32)
            mine = contrib[b, head, rows]
            theirs = xc_recv[b, head, rows].astype(F32)
            p_out[b, head, rows] = (carried + jnp.where(first, mine, 0.0)).astype(BF16)
            state[b, core * half + head, rows] = (carried + jnp.where(first, 0.0, theirs)).astype(BF16)

        pair_state(b).start()

    def pair_state(b):
        heads = pl.ds(core * half, half)
        return remote(p_out.at[b], state.at[b, heads], x_ss.at[2 * b + 1], x_rs.at[2 * b + 1], (mate, f))

    def state_wait(b):
        heads = pl.ds((1 - core) * half, half)
        remote(p_out.at[b], state.at[b, heads], x_ss.at[2 * b + 1], x_rs.at[2 * b + 1], (mate, f)).wait_recv()

    def q_of(h):
        return q_ref[:, head_cols(h)]

    def k_of(h):
        return k_ref[:, head_cols(h)]

    def v_of(h):
        return v_ref[:, head_cols(h)]

    def g_of(h):
        return gbuf[h // 2, :, pl.ds(pl.multiple_of((h % 2) * HEAD_DIM, HEAD_DIM), HEAD_DIM)]

    pair_start(0, k_of, v_of)
    og_all[f] = og_ref[...]
    sum_start(0)

    def g_copy(slot):
        return remote(gsend.at[slot], gbuf.at[f], g_ss.at[slot], g_rs.at[f], (s, slot))

    def g_make(slot):
        gsend[slot] = dot(og_all[slot], w_ref[...]).astype(BF16)
        g_copy(slot).start()

    gbuf[f] = dot(og_ref[...], w_ref[...]).astype(BF16)

    row_index = lax.broadcasted_iota(jnp.int32, (BLOCK, BLOCK), 0)
    col_index = lax.broadcasted_iota(jnp.int32, (BLOCK, BLOCK), 1)
    lower = row_index >= col_index
    upper = row_index <= col_index

    @pl.loop(0, HEADS // 2)
    def _(i):
        for u in range(2):
            h = 2 * i + u
            scores = jnp.where(lower, dot(q_of(h), k_of(h), NT), 0.0).astype(BF16)
            acc_a[:, head_cols(h)] = dot(scores, v_of(h))

    ag_full(0, down + xl, f).wait_recv()
    ag_half(3, down + xl, 0, up + xl).start()
    ag_full(0, up + xl, f).wait_recv()
    ag_half(4, up + xl, 1, down + xl).start()
    ag_full(0, xp, f).wait_recv()
    ag_full(5, xp, up + xl).start()
    ag_full(6, xp, down + xl).start()
    g_make(down + xl)
    g_make(up + xl)
    g_make(xp)

    run_start(0, False)

    ag_half(0, far + xl, 0, f).wait_recv()
    ag_half(0, far + xl, 1, f).wait_recv()
    ag_full(7, far + xl, xp).start()
    g_make(far + xl)

    state_start(0, False)
    state_wait(0)

    def at_copy(slot):
        return remote(att_send.at[slot], att_all.at[f], at_ss.at[slot], at_rs.at[f], (s, slot))

    @pl.loop(0, HEADS // 2)
    def _(i):
        for u in range(2):
            h = 2 * i + u
            attended = dot(q_of(h), state[0, h]) + acc_a[:, head_cols(h)]
            att_send[i, :, u * HEAD_DIM:(u + 1) * HEAD_DIM] = (factor * attended).astype(BF16)

    att_all[f] = att_send[f]

    @pl.loop(1, group)
    def _(j):
        at_copy((f + j) % group).start()

    ag_full(0, down + ol, f).wait_recv()
    g_make(down + ol)
    ag_full(0, up + ol, f).wait_recv()
    g_make(up + ol)
    ag_full(0, far + ol, f).wait_recv()
    g_make(far + ol)

    @pl.loop(1, group)
    def _(j):
        slot = (f + j) % group
        remote(gsend.at[slot], gbuf.at[slot], g_ss.at[slot], g_rs.at[slot], (s, slot)).wait_recv()

    pair_start(1, q_of, g_of)
    sum_start(1)

    @pl.loop(0, HEADS // 2)
    def _(i):
        for u in range(2):
            h = 2 * i + u
            q, k, v, g = q_of(h), k_of(h), v_of(h), g_of(h)
            mixing = jnp.where(lower, dot(g, v, NT), 0.0).astype(BF16)
            grad = dot(mixing, k) + dot(g, state[0, h], NT)
            qg_ref[:, head_cols(h)] = (factor * grad).astype(BF16)
            mixing_t = jnp.where(upper, dot(v, g, NT), 0.0).astype(BF16)
            acc_k[:, head_cols(h)] = dot(mixing_t, q)
            scores_t = jnp.where(upper, dot(k, q, NT), 0.0).astype(BF16)
            acc_v[:, head_cols(h)] = dot(scores_t, g)

    run_start(1, True)

    @pl.loop(1, group)
    def _(j):
        slot = (f + j) % group
        remote(att_send.at[slot], att_all.at[slot], at_ss.at[slot], at_rs.at[slot], (s, slot)).wait_recv()

    depth, width = w_ref.shape
    out_rows = wg_ref.shape[0]
    step = 256
    rows_all = group * BLOCK

    @pl.loop(0, depth // step)
    def _(i):
        cols = pl.ds(pl.multiple_of(i * step, step), step)
        left = og_all[:, :, cols].reshape(rows_all, step)
        piece = dot(left, att_all[...].reshape(rows_all, width), TN)
        for n in range(step // (2 * out_rows)):
            at = i * (step // (2 * out_rows)) + n
            base = n * 2 * out_rows
            for c in range(2):
                rows = piece[base + c * out_rows:base + (c + 1) * out_rows]
                part[c, at] = rows

    @pl.loop(0, chips)
    def _(j):
        wx_send[j] = part[1 - core, j].astype(BF16)

    w_pair = remote(wx_send, wx_recv, x_ss.at[4], x_rs.at[4], (mate, f))
    w_pair.start()

    state_start(1, True)

    w_pair.wait_recv()

    @pl.loop(0, chips)
    def _(j):
        wa_send[j] = (part[core, j] + wx_recv[j].astype(F32)).astype(BF16)

    wa_recv[chip] = wa_send[chip]
    a2a_start(wa_send, wa_recv, 4)

    state_wait(1)

    @pl.loop(0, HEADS // 2)
    def _(i):
        for u in range(2):
            h = 2 * i + u
            after = state[1, h]
            grad = dot(v_of(h), after, NT) + acc_k[:, head_cols(h)]
            kg_ref[:, head_cols(h)] = (factor * grad).astype(BF16)
            grad = dot(k_of(h), after) + acc_v[:, head_cols(h)]
            vg_ref[:, head_cols(h)] = (factor * grad).astype(BF16)

    a2a_wait(wa_send, wa_recv, 4)
    total = wa_recv[0].astype(F32)
    for j in range(1, chips):
        total = total + wa_recv[j].astype(F32)
    wg_ref[...] = total * grad_factor

    ag_own(0, up + xl).wait_send()
    ag_own(1, down + xl).wait_send()
    ag_own(2, xp).wait_send()
    ag_half(3, down + xl, 0, up + xl).wait_send()
    ag_half(4, up + xl, 1, down + xl).wait_send()
    ag_full(5, xp, up + xl).wait_send()
    ag_full(6, xp, down + xl).wait_send()
    ag_full(7, far + xl, xp).wait_send()

    @pl.loop(1, group)
    def _(j):
        slot = (f + j) % group
        g_copy(slot).wait_send()
        at_copy(slot).wait_send()

    for b in range(2):
        remote(xc_send.at[b], xc_recv.at[b], x_ss.at[2 * b], x_rs.at[2 * b], (mate, f)).wait_send()
        pair_state(b).wait_send()
        a2a_drain(a_send.at[b], a_recv.at[b], 2 * b)
        a2a_drain(r_send.at[b], r_recv.at[b], 2 * b + 1)
    w_pair.wait_send()
    a2a_drain(wa_send, wa_recv, 4)


def body(queries, key_vectors, value_vectors, out_grad, out_weight):
    seq_devices = lax.axis_size("seq")
    group = lax.axis_size("fsdp")
    chips = seq_devices // 2
    _, tokens, width_all = queries.shape
    depth, width = out_weight.shape
    factor = 1.0 / math.sqrt(HEAD_DIM * tokens * seq_devices)
    grad_factor = 1.0 / math.sqrt(group * tokens * seq_devices)
    half = HEADS // 2
    out_rows = depth // seq_devices
    slice_rows = half * HEAD_DIM // chips
    flat = (tokens, width_all)
    vmem = pl.BlockSpec(memory_space=pltpu.VMEM)
    slices = pltpu.VMEM((2, chips, slice_rows, HEAD_DIM), BF16)
    half_low = pltpu.VMEM((2, half, HEAD_DIM, HEAD_DIM), BF16)
    pieces = pltpu.VMEM((chips, out_rows, width), BF16)
    blocks = pltpu.VMEM((group, tokens, width), BF16)
    dma = pltpu.SemaphoreType.DMA
    results = pl.pallas_call(
        functools.partial(kernel, chips, group // 2, factor, grad_factor),
        out_shape=(
            jax.ShapeDtypeStruct(flat, BF16),
            jax.ShapeDtypeStruct(flat, BF16),
            jax.ShapeDtypeStruct(flat, BF16),
            jax.ShapeDtypeStruct((out_rows, width), F32),
        ),
        in_specs=[vmem] * 5,
        out_specs=(vmem,) * 4,
        scratch_shapes=[
            pltpu.VMEM((group, tokens, depth), BF16),
            blocks,
            blocks,
            blocks,
            blocks,
            pltpu.VMEM((2, half, HEAD_DIM, HEAD_DIM), F32),
            half_low,
            half_low,
            slices,
            slices,
            slices,
            slices,
            half_low,
            pltpu.VMEM((2, HEADS, HEAD_DIM, HEAD_DIM), BF16),
            pltpu.VMEM(flat, F32),
            pltpu.VMEM(flat, F32),
            pltpu.VMEM(flat, F32),
            pltpu.VMEM((2, chips, out_rows, width), F32),
            pieces,
            pieces,
            pieces,
            pieces,
            dma((8,)),
            dma((group, 2)),
            dma((group,)),
            dma((group,)),
            dma((group,)),
            dma((group,)),
            dma((5,)),
            dma((5,)),
            dma((5, chips)),
            dma((5, chips)),
        ],
        compiler_params=pltpu.CompilerParams(
            collective_id=0, has_side_effects=True, vmem_limit_bytes=48 * 1024 * 1024
        ),
    )(
        queries.reshape(flat),
        key_vectors.reshape(flat),
        value_vectors.reshape(flat),
        out_grad.reshape(flat),
        out_weight,
    )
    whole = (1,) + flat
    return (
        results[0].reshape(whole),
        results[1].reshape(whole),
        results[2].reshape(whole),
        results[3],
    )


def solution(mesh):
    in_specs = (
        P("fsdp", "seq", None),
        P("fsdp", "seq", None),
        P("fsdp", "seq", None),
        P("fsdp", "seq", None),
        P(None, "fsdp"),
    )
    out_specs = (
        P("fsdp", "seq", None),
        P("fsdp", "seq", None),
        P("fsdp", "seq", None),
        P("seq", "fsdp"),
    )
    return jax.shard_map(body, mesh=mesh, in_specs=in_specs, out_specs=out_specs, check_vma=False)
```

```python
import functools
import math

import jax
import jax.numpy as jnp
from jax import lax
from jax.experimental import pallas as pl
from jax.experimental.pallas import tpu as pltpu
from jax.sharding import PartitionSpec as P

HEADS = 16
HEAD_DIM = 128
BLOCK = 128
MESH = pl.DeviceIdType.MESH
F32 = jnp.float32
BF16 = jnp.bfloat16
NT = (((1,), (1,)), ((), ()))
TN = (((0,), (0,)), ((), ()))


def dot(a, b, dims=(((1,), (0,)), ((), ()))):
    return lax.dot_general(a, b, dims, preferred_element_type=F32)


def head_cols(h):
    return pl.ds(pl.multiple_of(h * HEAD_DIM, HEAD_DIM), HEAD_DIM)


def kernel(
    chips,
    ring,
    factor,
    grad_factor,
    q_in,
    k_in,
    v_in,
    og_in,
    w_in,
    qg_ref,
    kg_ref,
    vg_ref,
    wg_ref,
    q_ref,
    k_ref,
    v_ref,
    w_ref,
    og_all,
    gbuf,
    gsend,
    att_all,
    att_send,
    contrib0,
    xc_send0,
    xc_recv0,
    slices0,
    p_out0,
    contrib1,
    xc_send1,
    xc_recv1,
    slices1,
    p_out1,
    state,
    acc_a,
    acc_k,
    acc_v,
    part,
    wp_send,
    wp_recv,
    wx_send,
    wx_recv,
    wz_send,
    wz_recv,
    in_sem,
    ag_ss,
    ag_rs,
    g_ss,
    g_rs,
    at_ss,
    at_rs,
    x_ss,
    x_rs,
    a_ss,
    a_rs,
    w_ss,
    w_rs,
):
    s = lax.axis_index("seq")
    f = lax.axis_index("fsdp")
    group = 2 * ring
    half = HEADS // 2
    chip, core = s // 2, s % 2
    mate = s + 1 - 2 * core
    yy, xl = f // 2, f % 2
    xp = f + 1 - 2 * xl
    up = ((yy + 1) % ring) * 2
    down = ((yy + ring - 1) % ring) * 2
    far = ((yy + 2) % ring) * 2
    ol = 1 - xl

    def remote(src, dst, ssem, rsem, dev):
        return pltpu.make_async_remote_copy(
            src_ref=src,
            dst_ref=dst,
            send_sem=ssem,
            recv_sem=rsem,
            device_id=dev,
            device_id_type=MESH,
        )

    load_k = pltpu.make_async_copy(k_in, k_ref, in_sem.at[0])
    load_v = pltpu.make_async_copy(v_in, v_ref, in_sem.at[1])
    load_og = pltpu.make_async_copy(og_in, og_all.at[f], in_sem.at[2])
    load_w = pltpu.make_async_copy(w_in, w_ref, in_sem.at[3])
    load_q = pltpu.make_async_copy(q_in, q_ref, in_sem.at[4])
    for load in (load_k, load_v, load_og, load_w, load_q):
        load.start()
    barrier = pltpu.get_barrier_semaphore()

    @pl.loop(1, group)
    def _(j):
        pl.semaphore_signal(barrier, inc=1, device_id=(s, (f + j) % group), device_id_type=MESH)

    @pl.loop(1, chips)
    def _(j):
        other = ((chip + j) % chips) * 2 + core
        pl.semaphore_signal(barrier, inc=1, device_id=(other, f), device_id_type=MESH)

    pl.semaphore_signal(barrier, inc=1, device_id=(mate, f), device_id_type=MESH)
    pl.semaphore_wait(barrier, group - 1 + chips - 1 + 1)

    def half_view(ref, part_at):
        return ref.at[pl.ds(part_at * (BLOCK // 2), BLOCK // 2)]

    def ag_own(n, part_at, dev):
        return remote(
            half_view(og_in, part_at), half_view(og_all.at[f], part_at),
            ag_ss.at[n, part_at], ag_rs.at[f, part_at], (s, dev),
        )

    def ag_pass(n, slot, part_at, dev):
        view = half_view(og_all.at[slot], part_at)
        return remote(view, view, ag_ss.at[n, part_at], ag_rs.at[slot, part_at], (s, dev))

    def ag_wait(slot, part_at):
        ag_pass(0, slot, part_at, xp).wait_recv()

    for part_at in range(2):
        ag_own(0, part_at, up + xl).start()
        ag_own(1, 1 - part_at, down + xl).start()
        ag_own(2, part_at, xp).start()

    def q_of(h):
        return q_ref[:, head_cols(h)]

    def k_of(h):
        return k_ref[:, head_cols(h)]

    def v_of(h):
        return v_ref[:, head_cols(h)]

    def g_of(h):
        return gbuf[h // 2, :, pl.ds(pl.multiple_of((h % 2) * HEAD_DIM, HEAD_DIM), HEAD_DIM)]

    def a2a_copy(src, dst, n, there):
        return remote(src, dst, a_ss.at[n], a_rs.at[n], (there * 2 + core, f))

    def a2a_start(src, dst, n):
        @pl.loop(1, chips)
        def _(j):
            there = (chip + j) % chips
            a2a_copy(src.at[there], dst.at[chip], n, there).start()

    def a2a_all(src, dst, n):
        every = pl.ds(0, chips - 1)
        return remote(src.at[every], dst.at[every], a_ss.at[n], a_rs.at[n], (mate, f))

    def a2a_wait(src, dst, n):
        a2a_all(src, dst, n).wait_recv()

    def a2a_drain(src, dst, n):
        a2a_all(src, dst, n).wait_send()

    class Scan:
        def __init__(self, at, b, reverse, mine, other, left, right, bufs):
            self.at, self.b, self.reverse = at, b, reverse
            self.mine, self.other, self.left, self.right = mine, other, left, right
            self.contrib, self.xc_send, self.xc_recv, slices, self.p_out = bufs
            self.a_send, self.a_recv, self.r_send, self.r_recv = [slices.at[i] for i in range(4)]
            self.heads = self.contrib.shape[0]
            self.rows = self.heads * HEAD_DIM // chips

        def pair(self):
            return remote(
                self.xc_send, self.xc_recv, x_ss.at[2 * self.at], x_rs.at[2 * self.at], (mate, f)
            )

        def place(self, j):
            row = pl.multiple_of((j * self.rows) % HEAD_DIM, self.rows)
            return j * self.rows // HEAD_DIM, pl.ds(row, self.rows)

        def start(self):
            @pl.loop(0, self.heads // 2)
            def _(i):
                for u in range(2):
                    h = self.other + 2 * i + u
                    self.xc_send[2 * i + u] = dot(self.left(h), self.right(h), TN)

            self.pair().start()

            @pl.loop(0, self.heads // 2)
            def _(i):
                for u in range(2):
                    h = self.mine + 2 * i + u
                    self.contrib[2 * i + u] = dot(self.left(h), self.right(h), TN)

        def spread(self):
            self.pair().wait_recv()

            @pl.loop(0, chips)
            def _(j):
                head, rows = self.place(j)
                self.a_send[j] = (self.contrib[head, rows] + self.xc_recv[head, rows]).astype(BF16)

            self.a_recv[chip] = self.a_send[chip]
            a2a_start(self.a_send, self.a_recv, 2 * self.at)

        def run(self):
            a2a_wait(self.a_send, self.a_recv, 2 * self.at)
            total = jnp.zeros((self.rows, HEAD_DIM), F32)
            for j in range(chips):
                at = chips - 1 - j if self.reverse else j
                self.r_send[at] = total.astype(BF16)
                total = total + self.a_recv[at].astype(F32)
            self.r_recv[chip] = self.r_send[chip]
            a2a_start(self.r_send, self.r_recv, 2 * self.at + 1)

        def back(self):
            heads = pl.ds(self.mine, self.heads)
            return remote(
                self.p_out, state.at[self.b, heads],
                x_ss.at[2 * self.at + 1], x_rs.at[2 * self.at + 1], (mate, f),
            )

        def finish(self):
            a2a_wait(self.r_send, self.r_recv, 2 * self.at + 1)
            first = core == (1 if self.reverse else 0)

            @pl.loop(0, chips)
            def _(j):
                head, rows = self.place(j)
                carried = self.r_recv[j].astype(F32)
                mine, theirs = self.contrib[head, rows], self.xc_recv[head, rows]
                self.p_out[head, rows] = (carried + jnp.where(first, mine, 0.0)).astype(BF16)
                state[self.b, self.mine + head, rows] = (
                    carried + jnp.where(first, 0.0, theirs)
                ).astype(BF16)

            self.back().start()

        def wait(self):
            heads = pl.ds(self.other, self.heads)
            remote(
                self.p_out, state.at[self.b, heads],
                x_ss.at[2 * self.at + 1], x_rs.at[2 * self.at + 1], (mate, f),
            ).wait_recv()

        def drain(self):
            self.pair().wait_send()
            self.back().wait_send()
            a2a_drain(self.a_send, self.a_recv, 2 * self.at)
            a2a_drain(self.r_send, self.r_recv, 2 * self.at + 1)

    kv = Scan(
        0, 0, False, core * half, (1 - core) * half, k_of, v_of,
        (contrib0, xc_send0, xc_recv0, slices0, p_out0),
    )
    pairs = ((f, xp), (down + xl, up + xl), (down + ol, up + ol), (far + xl, far + ol))
    qg = []
    for n, (first, second) in enumerate(pairs):
        mine = 2 * (first + core * (second - first))
        other = 2 * (second + core * (first - second))
        bufs = tuple(ref.at[n] for ref in (contrib1, xc_send1, xc_recv1, slices1, p_out1))
        qg.append(Scan(1 + n, 1, True, mine, other, q_of, g_of, bufs))

    load_k.wait()
    load_v.wait()
    kv.start()
    kv.spread()

    def g_copy(slot):
        return remote(gsend.at[slot], gbuf.at[f], g_ss.at[slot], g_rs.at[f], (s, slot))

    def g_make(slot):
        gsend[slot] = dot(og_all[slot], w_ref[...]).astype(BF16)
        g_copy(slot).start()

    def g_wait(slot):
        remote(gsend.at[slot], gbuf.at[slot], g_ss.at[slot], g_rs.at[slot], (s, slot)).wait_recv()

    load_og.wait()
    load_w.wait()
    gbuf[f] = dot(og_all[f], w_ref[...]).astype(BF16)

    row_index = lax.broadcasted_iota(jnp.int32, (BLOCK, BLOCK), 0)
    col_index = lax.broadcasted_iota(jnp.int32, (BLOCK, BLOCK), 1)
    lower = row_index >= col_index
    upper = row_index <= col_index
    load_q.wait()

    @pl.loop(0, HEADS // 2)
    def _(i):
        for u in range(2):
            h = 2 * i + u
            scores = jnp.where(lower, dot(q_of(h), k_of(h), NT), 0.0).astype(BF16)
            acc_a[:, head_cols(h)] = dot(scores, v_of(h))

    ag_wait(down + xl, 0)
    ag_pass(3, down + xl, 0, up + xl).start()
    ag_wait(up + xl, 1)
    ag_pass(3, up + xl, 1, down + xl).start()
    ag_wait(xp, 0)
    ag_pass(4, xp, 0, up + xl).start()
    ag_pass(5, xp, 0, down + xl).start()
    ag_wait(xp, 1)
    ag_pass(4, xp, 1, up + xl).start()
    ag_pass(5, xp, 1, down + xl).start()
    g_make(xp)
    kv.run()
    ag_wait(down + xl, 1)
    g_make(down + xl)
    ag_wait(up + xl, 0)
    g_make(up + xl)
    ag_wait(far + xl, 0)
    ag_pass(6, far + xl, 0, xp).start()
    ag_wait(far + xl, 1)
    ag_pass(6, far + xl, 1, xp).start()
    g_make(far + xl)

    def local_grads(h):
        q, k, v, g = q_of(h), k_of(h), v_of(h), g_of(h)
        mixing = jnp.where(lower, dot(g, v, NT), 0.0).astype(BF16)
        grad = dot(mixing, k) + dot(g, state[0, h], NT)
        qg_ref[:, head_cols(h)] = (factor * grad).astype(BF16)
        mixing_t = jnp.where(upper, dot(v, g, NT), 0.0).astype(BF16)
        acc_k[:, head_cols(h)] = dot(mixing_t, q)
        scores_t = jnp.where(upper, dot(k, q, NT), 0.0).astype(BF16)
        acc_v[:, head_cols(h)] = dot(scores_t, g)

    def local_pair(n):
        for column in pairs[n]:
            for u in range(2):
                local_grads(2 * column + u)

    def at_copy(slot):
        return remote(att_send.at[slot], att_all.at[f], at_ss.at[0], at_rs.at[0], (s, slot))

    def at_all():
        every = pl.ds(0, group - 1)
        return remote(att_send.at[every], att_all.at[every], at_ss.at[0], at_rs.at[0], (mate, f))

    g_wait(xp)
    qg[0].start()
    qg[0].spread()
    kv.finish()
    kv.wait()
    @pl.loop(0, HEADS // 2)
    def _(i):
        for u in range(2):
            h = 2 * i + u
            attended = dot(q_of(h), state[0, h]) + acc_a[:, head_cols(h)]
            att_send[i, :, u * HEAD_DIM:(u + 1) * HEAD_DIM] = (factor * attended).astype(BF16)

    att_all[f] = att_send[f]

    @pl.loop(1, group)
    def _(j):
        at_copy((f + j) % group).start()

    local_pair(0)
    ag_wait(down + ol, 0)
    ag_wait(down + ol, 1)
    g_make(down + ol)
    ag_wait(up + ol, 0)
    ag_wait(up + ol, 1)
    g_make(up + ol)
    ag_wait(far + ol, 0)
    ag_wait(far + ol, 1)
    g_make(far + ol)
    qg[0].run()
    g_wait(down + xl)
    g_wait(up + xl)
    qg[1].start()
    qg[1].spread()
    local_pair(1)

    at_all().wait_recv()

    depth, width = w_ref.shape
    out_rows = wg_ref.shape[0]
    step = 256
    rows_all = group * BLOCK

    @pl.loop(0, depth // step)
    def _(i):
        cols = pl.ds(pl.multiple_of(i * step, step), step)
        left = og_all[:, :, cols].reshape(rows_all, step)
        piece = dot(left, att_all[...].reshape(rows_all, width), TN)
        for n in range(2):
            for c in range(2):
                base = (2 * n + c) * out_rows
                part[c, n, i] = piece[base:base + out_rows]

    levels = chips // 2
    z, xh = chip // 2, chip % 2
    across = (2 * z + 1 - xh) * 2 + core
    quarter = out_rows // 2

    def w_rows(p):
        return pl.ds(p * quarter, quarter)

    def w_pair(p):
        return remote(wp_send.at[p], wp_recv.at[p], w_ss.at[p], w_rs.at[p], (mate, f))

    def w_cross(p):
        return remote(wx_send.at[p], wx_recv.at[p], w_ss.at[2 + p], w_rs.at[2 + p], (across, f))

    def w_level(p, there):
        to = (2 * there + xh) * 2 + core
        return remote(wz_send.at[p, there], wz_recv.at[p, z], w_ss.at[4 + p], w_rs.at[4 + p], (to, f))

    def w_levels(p):
        every = pl.ds(0, levels - 1)
        return remote(
            wz_send.at[p, every], wz_recv.at[p, every], w_ss.at[4 + p], w_rs.at[4 + p], (mate, f)
        )

    def w_pair_start(p):
        @pl.loop(0, levels)
        def _(j):
            for n in range(2):
                wp_send[p, n, j] = part[1 - core, n, j, w_rows(p)].astype(BF16)

        w_pair(p).start()

    def w_cross_start(p):
        w_pair(p).wait_recv()

        @pl.loop(0, levels)
        def _(j):
            total = part[core, 1 - xh, j, w_rows(p)] + wp_recv[p, 1 - xh, j].astype(F32)
            wx_send[p, j] = total.astype(BF16)

        w_cross(p).start()

    def w_level_start(p):
        w_cross(p).wait_recv()

        @pl.loop(0, levels)
        def _(j):
            total = part[core, xh, j, w_rows(p)] + wp_recv[p, xh, j].astype(F32)
            wz_send[p, j] = (total + wx_recv[p, j].astype(F32)).astype(BF16)

        wz_recv[p, z] = wz_send[p, z]

        @pl.loop(1, levels)
        def _(j):
            w_level(p, (z + j) % levels).start()

    def w_finish(p):
        w_levels(p).wait_recv()
        total = wz_recv[p, 0].astype(F32)
        for j in range(1, levels):
            total = total + wz_recv[p, j].astype(F32)
        wg_ref[w_rows(p)] = total * grad_factor

    w_pair_start(0)
    w_pair_start(1)
    g_wait(down + ol)
    g_wait(up + ol)
    qg[2].start()
    w_cross_start(0)
    w_cross_start(1)
    qg[2].spread()
    g_wait(far + xl)
    g_wait(far + ol)
    qg[3].start()
    qg[3].spread()
    qg[1].run()
    local_pair(2)
    w_level_start(0)
    local_pair(3)
    qg[2].run()
    w_level_start(1)
    qg[3].run()

    def final_pair(n):
        for column in pairs[n]:
            for u in range(2):
                h = 2 * column + u
                after = state[1, h]
                grad = dot(v_of(h), after, NT) + acc_k[:, head_cols(h)]
                kg_ref[:, head_cols(h)] = (factor * grad).astype(BF16)
                grad = dot(k_of(h), after) + acc_v[:, head_cols(h)]
                vg_ref[:, head_cols(h)] = (factor * grad).astype(BF16)

    qg[0].finish()
    qg[1].finish()
    for n in range(2):
        qg[n].wait()
        final_pair(n)
    qg[2].finish()
    qg[3].finish()
    for n in range(2, 4):
        qg[n].wait()
        final_pair(n)

    for part_at in range(2):
        ag_own(0, part_at, up + xl).wait_send()
        ag_own(1, part_at, down + xl).wait_send()
        ag_own(2, part_at, xp).wait_send()
        for n in range(3, 7):
            ag_pass(n, xp, part_at, xp).wait_send()

    @pl.loop(1, group)
    def _(j):
        g_copy((f + j) % group).wait_send()

    at_all().wait_send()
    kv.drain()
    for scan in qg:
        scan.drain()
    for p in range(2):
        w_pair(p).wait_send()
        w_cross(p).wait_send()
    for p in range(2):
        w_finish(p)
        w_levels(p).wait_send()


def store(*refs):
    sems = refs[-1]
    copies = [pltpu.make_async_copy(refs[i], refs[4 + i], sems.at[i]) for i in range(4)]
    for copy in copies:
        copy.start()
    for copy in copies:
        copy.wait()


def body(queries, key_vectors, value_vectors, out_grad, out_weight):
    seq_devices = lax.axis_size("seq")
    group = lax.axis_size("fsdp")
    chips = seq_devices // 2
    _, tokens, width_all = queries.shape
    depth, width = out_weight.shape
    factor = 1.0 / math.sqrt(HEAD_DIM * tokens * seq_devices)
    grad_factor = 1.0 / math.sqrt(group * tokens * seq_devices)
    half = HEADS // 2
    out_rows = depth // seq_devices
    flat = (tokens, width_all)
    vmem = pl.BlockSpec(memory_space=pltpu.VMEM)
    levels = chips // 2
    pieces = (levels, out_rows // 2, width)
    blocks = pltpu.VMEM((group, tokens, width), BF16)
    square = (HEAD_DIM, HEAD_DIM)
    chunk = (4, 2)
    dma = pltpu.SemaphoreType.DMA
    shapes = (
        jax.ShapeDtypeStruct(flat, BF16),
        jax.ShapeDtypeStruct(flat, BF16),
        jax.ShapeDtypeStruct(flat, BF16),
        jax.ShapeDtypeStruct((out_rows, width), F32),
    )
    args = [x.reshape(flat) for x in (queries, key_vectors, value_vectors, out_grad)]
    args = [pltpu.with_memory_space_constraint(x, pltpu.HBM) for x in (*args, out_weight)]
    results = pl.pallas_call(
        functools.partial(kernel, chips, group // 2, factor, grad_factor),
        out_shape=shapes,
        in_specs=[pl.BlockSpec(memory_space=pltpu.HBM)] * 5,
        out_specs=(vmem,) * 4,
        scratch_shapes=[
            pltpu.VMEM(flat, BF16),
            pltpu.VMEM(flat, BF16),
            pltpu.VMEM(flat, BF16),
            pltpu.VMEM((depth, width), BF16),
            pltpu.VMEM((group, tokens, depth), BF16),
            blocks,
            blocks,
            blocks,
            blocks,
            pltpu.VMEM((half,) + square, F32),
            pltpu.VMEM((half,) + square, F32),
            pltpu.VMEM((half,) + square, F32),
            pltpu.VMEM((4, chips, half * HEAD_DIM // chips, HEAD_DIM), BF16),
            pltpu.VMEM((half,) + square, BF16),
            pltpu.VMEM(chunk + square, F32),
            pltpu.VMEM(chunk + square, F32),
            pltpu.VMEM(chunk + square, F32),
            pltpu.VMEM((4, 4, chips, 2 * HEAD_DIM // chips, HEAD_DIM), BF16),
            pltpu.VMEM(chunk + square, BF16),
            pltpu.VMEM((2, HEADS) + square, BF16),
            pltpu.VMEM(flat, F32),
            pltpu.VMEM(flat, F32),
            pltpu.VMEM(flat, F32),
            pltpu.VMEM((2, 2, levels, out_rows, width), F32),
            pltpu.VMEM((2, 2) + pieces, BF16),
            pltpu.VMEM((2, 2) + pieces, BF16),
            pltpu.VMEM((2,) + pieces, BF16),
            pltpu.VMEM((2,) + pieces, BF16),
            pltpu.VMEM((2,) + pieces, BF16),
            pltpu.VMEM((2,) + pieces, BF16),
            dma((5,)),
            dma((7, 2)),
            dma((group, 2)),
            dma((group,)),
            dma((group,)),
            dma((1,)),
            dma((1,)),
            dma((10,)),
            dma((10,)),
            dma((10,)),
            dma((10,)),
            dma((6,)),
            dma((6,)),
        ],
        compiler_params=pltpu.CompilerParams(
            collective_id=0, has_side_effects=True, vmem_limit_bytes=44 * 1024 * 1024
        ),
    )(*args)
    results = pl.pallas_call(
        store,
        out_shape=shapes,
        in_specs=[vmem] * 4,
        out_specs=(pl.BlockSpec(memory_space=pltpu.HBM),) * 4,
        scratch_shapes=[dma((4,))],
        compiler_params=pltpu.CompilerParams(vmem_limit_bytes=16 * 1024 * 1024),
    )(*results)
    whole = (1,) + flat
    return (
        results[0].reshape(whole),
        results[1].reshape(whole),
        results[2].reshape(whole),
        results[3],
    )


def solution(mesh):
    in_specs = (
        P("fsdp", "seq", None),
        P("fsdp", "seq", None),
        P("fsdp", "seq", None),
        P("fsdp", "seq", None),
        P(None, "fsdp"),
    )
    out_specs = (
        P("fsdp", "seq", None),
        P("fsdp", "seq", None),
        P("fsdp", "seq", None),
        P("seq", "fsdp"),
    )
    return jax.shard_map(body, mesh=mesh, in_specs=in_specs, out_specs=out_specs, check_vma=False)
```

```python
import functools
import math

import jax
import jax.numpy as jnp
from jax import lax
from jax.experimental import pallas as pl
from jax.experimental.pallas import tpu as pltpu
from jax.sharding import PartitionSpec as P

HEADS = 16
HEAD_DIM = 128
BLOCK = 128
MESH = pl.DeviceIdType.MESH
F32 = jnp.float32
BF16 = jnp.bfloat16
NT = (((1,), (1,)), ((), ()))
TN = (((0,), (0,)), ((), ()))


def dot(a, b, dims=(((1,), (0,)), ((), ()))):
    return lax.dot_general(a, b, dims, preferred_element_type=F32)


def head_cols(h):
    return pl.ds(pl.multiple_of(h * HEAD_DIM, HEAD_DIM), HEAD_DIM)


def kernel(
    chips,
    ring,
    factor,
    grad_factor,
    q_in,
    k_in,
    v_in,
    og_in,
    w_in,
    qg_ref,
    kg_ref,
    vg_ref,
    wg_ref,
    q_ref,
    k_ref,
    v_ref,
    w_all,
    og_all,
    gbuf,
    gsend,
    att_all,
    att_send,
    contrib0,
    xc_send0,
    xc_recv0,
    slices0,
    p_out0,
    contrib1,
    xc_send1,
    xc_recv1,
    slices1,
    p_out1,
    state,
    acc_a,
    acc_k,
    acc_v,
    part,
    wp_send,
    wp_recv,
    wx_send,
    wx_recv,
    wz_send,
    wz_recv,
    in_sem,
    ag_ss,
    ag_rs,
    g_ss,
    g_rs,
    at_ss,
    at_rs,
    x_ss,
    x_rs,
    a_ss,
    a_rs,
    w_ss,
    w_rs,
):
    s = lax.axis_index("seq")
    f = lax.axis_index("fsdp")
    group = 2 * ring
    half = HEADS // 2
    chip, core = s // 2, s % 2
    levels = chips // 2
    z, xh = chip // 2, chip % 2
    across = (2 * z + 1 - xh) * 2 + core
    mate = s + 1 - 2 * core
    yy, xl = f // 2, f % 2
    xp = f + 1 - 2 * xl
    up = ((yy + 1) % ring) * 2
    down = ((yy + ring - 1) % ring) * 2
    far = ((yy + 2) % ring) * 2
    ol = 1 - xl

    def remote(src, dst, ssem, rsem, dev):
        return pltpu.make_async_remote_copy(
            src_ref=src,
            dst_ref=dst,
            send_sem=ssem,
            recv_sem=rsem,
            device_id=dev,
            device_id_type=MESH,
        )

    load_k = pltpu.make_async_copy(k_in, k_ref, in_sem.at[0])
    load_v = pltpu.make_async_copy(v_in, v_ref, in_sem.at[1])
    load_og = pltpu.make_async_copy(og_in, og_all.at[f], in_sem.at[2])
    load_w = pltpu.make_async_copy(w_in, w_all.at[xl], in_sem.at[3])
    load_q = pltpu.make_async_copy(q_in, q_ref, in_sem.at[4])
    for load in (load_k, load_v, load_og, load_w, load_q):
        load.start()
    barrier = pltpu.get_barrier_semaphore()

    @pl.loop(1, group)
    def _(j):
        pl.semaphore_signal(barrier, inc=1, device_id=(s, (f + j) % group), device_id_type=MESH)

    @pl.loop(1, chips)
    def _(j):
        other = ((chip + j) % chips) * 2 + core
        pl.semaphore_signal(barrier, inc=1, device_id=(other, f), device_id_type=MESH)

    pl.semaphore_signal(barrier, inc=1, device_id=(mate, f), device_id_type=MESH)
    pl.semaphore_signal(barrier, inc=1, device_id=(across, xp), device_id_type=MESH)
    pl.semaphore_wait(barrier, group - 1 + chips - 1 + 2)

    def quarter_view(ref, part_at):
        return ref.at[pl.ds(part_at * (BLOCK // 4), BLOCK // 4)]

    def ag_own(n, part_at, dev):
        return remote(
            quarter_view(og_in, part_at), quarter_view(og_all.at[f], part_at),
            ag_ss.at[n, part_at], ag_rs.at[f, part_at], (s, dev),
        )

    def ag_pass(n, slot, part_at, dev):
        view = quarter_view(og_all.at[slot], part_at)
        return remote(view, view, ag_ss.at[n, part_at], ag_rs.at[slot, part_at], (s, dev))

    def ag_wait(slot, *parts_at):
        for part_at in parts_at:
            ag_pass(0, slot, part_at, xp).wait_recv()

    own = [ag_own(0, p, up + xl) for p in range(4)] + [ag_own(1, p, down + xl) for p in (3, 2, 1, 0)]
    own_across = [ag_own(2, p, xp) for p in range(4)]
    past_up = [ag_pass(3, down + xl, p, up + xl) for p in (0, 1)]
    past_down = [ag_pass(3, up + xl, p, down + xl) for p in (3, 2)]
    partner_up = {p: ag_pass(4, xp, p, up + xl) for p in (0, 1, 2)}
    partner_down = {p: ag_pass(5, xp, p, down + xl) for p in (1, 2, 3)}
    far_across = {p: ag_pass(6, far + xl, p, xp) for p in range(4)}
    down_across = ag_pass(7, down + xl, 3, xp)
    up_across = ag_pass(7, up + xl, 0, xp)

    w_part = w_in.shape[0] // 2
    w_rows_here = pl.ds(core * w_part, w_part)
    w_rows_mate = pl.ds((1 - core) * w_part, w_part)
    w_side = remote(
        w_in.at[w_rows_here], w_all.at[xl, w_rows_here], w_ss.at[6], w_rs.at[6], (across, xp)
    )
    w_got = w_all.at[1 - xl, w_rows_here]
    w_share = remote(w_got, w_got, w_ss.at[7], w_rs.at[7], (mate, f))

    w_side.start()
    for p in range(4):
        own[p].start()
        own[4 + p].start()
        if p < 2:
            own_across[p].start()

    def q_of(h):
        return q_ref[:, head_cols(h)]

    def k_of(h):
        return k_ref[:, head_cols(h)]

    def v_of(h):
        return v_ref[:, head_cols(h)]

    def g_of(h):
        return gbuf[h // 2, :, pl.ds(pl.multiple_of((h % 2) * HEAD_DIM, HEAD_DIM), HEAD_DIM)]

    def a2a_copy(src, dst, n, there):
        return remote(src, dst, a_ss.at[n], a_rs.at[n], (there * 2 + core, f))

    def a2a_start(src, dst, n):
        @pl.loop(1, chips)
        def _(j):
            there = (chip + j) % chips
            a2a_copy(src.at[there], dst.at[chip], n, there).start()

    def a2a_all(src, dst, n):
        every = pl.ds(0, chips - 1)
        return remote(src.at[every], dst.at[every], a_ss.at[n], a_rs.at[n], (mate, f))

    def a2a_wait(src, dst, n):
        a2a_all(src, dst, n).wait_recv()

    def a2a_drain(src, dst, n):
        a2a_all(src, dst, n).wait_send()

    class Scan:
        def __init__(self, at, b, reverse, mine, other, left, right, bufs):
            self.at, self.b, self.reverse = at, b, reverse
            self.mine, self.other, self.left, self.right = mine, other, left, right
            self.contrib, self.xc_send, self.xc_recv, slices, self.p_out = bufs
            self.a_send, self.a_recv, self.r_send, self.r_recv = [slices.at[i] for i in range(4)]
            self.heads = self.contrib.shape[0]
            self.rows = self.heads * HEAD_DIM // chips

        def pair(self):
            return remote(
                self.xc_send, self.xc_recv, x_ss.at[2 * self.at], x_rs.at[2 * self.at], (mate, f)
            )

        def place(self, j):
            row = pl.multiple_of((j * self.rows) % HEAD_DIM, self.rows)
            return j * self.rows // HEAD_DIM, pl.ds(row, self.rows)

        def start(self):
            @pl.loop(0, self.heads // 2)
            def _(i):
                for u in range(2):
                    h = self.other + 2 * i + u
                    self.xc_send[2 * i + u] = dot(self.left(h), self.right(h), TN)

            self.pair().start()

            @pl.loop(0, self.heads // 2)
            def _(i):
                for u in range(2):
                    h = self.mine + 2 * i + u
                    self.contrib[2 * i + u] = dot(self.left(h), self.right(h), TN)

        def spread(self):
            self.pair().wait_recv()

            @pl.loop(0, chips)
            def _(j):
                head, rows = self.place(j)
                self.a_send[j] = (self.contrib[head, rows] + self.xc_recv[head, rows]).astype(BF16)

            self.a_recv[chip] = self.a_send[chip]
            a2a_start(self.a_send, self.a_recv, 2 * self.at)

        def run(self):
            a2a_wait(self.a_send, self.a_recv, 2 * self.at)
            total = jnp.zeros((self.rows, HEAD_DIM), F32)
            for j in range(chips):
                at = chips - 1 - j if self.reverse else j
                self.r_send[at] = total.astype(BF16)
                total = total + self.a_recv[at].astype(F32)
            self.r_recv[chip] = self.r_send[chip]
            a2a_start(self.r_send, self.r_recv, 2 * self.at + 1)

        def back(self):
            heads = pl.ds(self.mine, self.heads)
            return remote(
                self.p_out, state.at[self.b, heads],
                x_ss.at[2 * self.at + 1], x_rs.at[2 * self.at + 1], (mate, f),
            )

        def finish(self):
            a2a_wait(self.r_send, self.r_recv, 2 * self.at + 1)
            first = core == (1 if self.reverse else 0)

            @pl.loop(0, chips)
            def _(j):
                head, rows = self.place(j)
                carried = self.r_recv[j].astype(F32)
                mine, theirs = self.contrib[head, rows], self.xc_recv[head, rows]
                self.p_out[head, rows] = (carried + jnp.where(first, mine, 0.0)).astype(BF16)
                state[self.b, self.mine + head, rows] = (
                    carried + jnp.where(first, 0.0, theirs)
                ).astype(BF16)

            self.back().start()

        def wait(self):
            heads = pl.ds(self.other, self.heads)
            remote(
                self.p_out, state.at[self.b, heads],
                x_ss.at[2 * self.at + 1], x_rs.at[2 * self.at + 1], (mate, f),
            ).wait_recv()

        def drain(self):
            self.pair().wait_send()
            self.back().wait_send()
            a2a_drain(self.a_send, self.a_recv, 2 * self.at)
            a2a_drain(self.r_send, self.r_recv, 2 * self.at + 1)

    kv = Scan(
        0, 0, False, core * half, (1 - core) * half, k_of, v_of,
        (contrib0, xc_send0, xc_recv0, slices0, p_out0),
    )
    pairs = tuple((row, row + 1) for row in (2 * yy, up, down, far))
    qg = []
    for n, (first, second) in enumerate(pairs):
        mine = 2 * (first + core * (second - first))
        other = 2 * (second + core * (first - second))
        bufs = tuple(ref.at[n] for ref in (contrib1, xc_send1, xc_recv1, slices1, p_out1))
        qg.append(Scan(1 + n, 1, True, mine, other, q_of, g_of, bufs))

    load_k.wait()
    load_v.wait()
    kv.start()
    kv.spread()
    own_across[2].start()
    own_across[3].start()

    def g_copy(n, row):
        to = gbuf.at[pl.ds(2 * yy, 2)]
        return remote(gsend.at[n], to, g_ss.at[n], g_rs.at[yy], (s, row + xl))

    def g_make(n, row):
        for c in range(2):
            gsend[n, c] = dot(og_all[row + xl], w_all[c]).astype(BF16)

    def g_wait(row):
        at = gbuf.at[pl.ds(row, 2)]
        remote(gsend.at[0], at, g_ss.at[0], g_rs.at[row // 2], (s, row + xl)).wait_recv()

    row_index = lax.broadcasted_iota(jnp.int32, (BLOCK, BLOCK), 0)
    col_index = lax.broadcasted_iota(jnp.int32, (BLOCK, BLOCK), 1)
    lower = row_index >= col_index
    upper = row_index <= col_index
    load_q.wait()

    @pl.loop(0, HEADS // 2)
    def _(i):
        for u in range(2):
            h = 2 * i + u
            scores = jnp.where(lower, dot(q_of(h), k_of(h), NT), 0.0).astype(BF16)
            acc_a[:, head_cols(h)] = dot(scores, v_of(h))

    for n in range(2):
        ag_wait(down + xl, n)
        past_up[n].start()
        ag_wait(up + xl, 3 - n)
        past_down[n].start()
    kv.run()
    for p in range(4):
        ag_wait(xp, p)
        if p < 3:
            partner_up[p].start()
        if p > 0:
            partner_down[p].start()
    ag_wait(down + xl, 2, 3)
    down_across.start()
    ag_wait(up + xl, 1, 0)
    up_across.start()
    remote(
        w_in.at[w_rows_here], w_got, w_ss.at[6], w_rs.at[6], (across, xp)
    ).wait_recv()
    w_share.start()
    load_og.wait()
    load_w.wait()
    w_theirs = w_all.at[1 - xl, w_rows_mate]
    remote(w_theirs, w_theirs, w_ss.at[7], w_rs.at[7], (mate, f)).wait_recv()
    for c in range(2):
        gbuf[2 * yy + c] = dot(og_all[f], w_all[c]).astype(BF16)
    g_make(0, up)
    g_copy(0, up).start()
    g_make(1, down)
    g_copy(1, down).start()
    for p in (0, 3, 1, 2):
        ag_wait(far + xl, p)
        far_across[p].start()

    def local_grads(h):
        q, k, v, g = q_of(h), k_of(h), v_of(h), g_of(h)
        mixing = jnp.where(lower, dot(g, v, NT), 0.0).astype(BF16)
        grad = dot(mixing, k) + dot(g, state[0, h], NT)
        qg_ref[:, head_cols(h)] = (factor * grad).astype(BF16)
        mixing_t = jnp.where(upper, dot(v, g, NT), 0.0).astype(BF16)
        acc_k[:, head_cols(h)] = dot(mixing_t, q)
        scores_t = jnp.where(upper, dot(k, q, NT), 0.0).astype(BF16)
        acc_v[:, head_cols(h)] = dot(scores_t, g)

    def local_pair(n):
        for column in pairs[n]:
            for u in range(2):
                local_grads(2 * column + u)

    def at_copy(slot):
        return remote(att_send.at[slot], att_all.at[f], at_ss.at[0], at_rs.at[0], (s, slot))

    def at_all():
        every = pl.ds(0, group - 1)
        return remote(att_send.at[every], att_all.at[every], at_ss.at[0], at_rs.at[0], (mate, f))

    qg[0].start()
    qg[0].spread()
    kv.finish()
    kv.wait()
    @pl.loop(0, HEADS // 2)
    def _(i):
        for u in range(2):
            h = 2 * i + u
            attended = dot(q_of(h), state[0, h]) + acc_a[:, head_cols(h)]
            att_send[i, :, u * HEAD_DIM:(u + 1) * HEAD_DIM] = (factor * attended).astype(BF16)

    att_all[f] = att_send[f]

    @pl.loop(1, group)
    def _(j):
        at_copy((f + j) % group).start()

    g_make(2, far)
    g_copy(2, far).start()
    local_pair(0)
    g_wait(up)
    qg[1].start()
    qg[1].spread()
    local_pair(1)
    g_wait(down)
    qg[2].start()
    qg[2].spread()
    local_pair(2)
    g_wait(far)
    qg[3].start()
    qg[3].spread()
    qg[0].run()
    local_pair(3)
    for row in (down, up, far):
        ag_wait(row + ol, 0, 1, 2, 3)

    at_all().wait_recv()

    depth, width = w_in.shape
    out_rows = wg_ref.shape[0]
    step = 256
    rows_all = group * BLOCK

    pairs_of_levels = levels // 2

    def w_part(p):
        @pl.loop(0, pairs_of_levels)
        def _(m):
            cols = pl.ds(pl.multiple_of((2 * m + p) * step, step), step)
            left = og_all[:, :, cols].reshape(rows_all, step)
            piece = dot(left, att_all[...].reshape(rows_all, width), TN)
            for n in range(2):
                for c in range(2):
                    base = (2 * n + c) * out_rows
                    part[c, n, p, m] = piece[base:base + out_rows]

    def w_pair(p):
        return remote(wp_send.at[p], wp_recv.at[p], w_ss.at[p], w_rs.at[p], (mate, f))

    def w_cross(p):
        return remote(wx_send.at[p], wx_recv.at[p], w_ss.at[2 + p], w_rs.at[2 + p], (across, f))

    def w_level(p, m):
        to = (2 * (2 * m + p) + xh) * 2 + core
        return remote(wz_send.at[p, m], wz_recv.at[z], w_ss.at[4], w_rs.at[4], (to, f))

    def w_levels():
        every = wz_recv.at[pl.ds(0, levels - 1)]
        return remote(every, every, w_ss.at[4], w_rs.at[4], (mate, f))

    def w_pair_start(p):
        @pl.loop(0, pairs_of_levels)
        def _(m):
            for n in range(2):
                wp_send[p, n, m] = part[1 - core, n, p, m].astype(BF16)

        w_pair(p).start()

    def w_cross_start(p):
        w_pair(p).wait_recv()

        @pl.loop(0, pairs_of_levels)
        def _(m):
            total = part[core, 1 - xh, p, m] + wp_recv[p, 1 - xh, m].astype(F32)
            wx_send[p, m] = total.astype(BF16)

        w_cross(p).start()

    def w_level_start(p):
        w_cross(p).wait_recv()

        @pl.loop(0, pairs_of_levels)
        def _(m):
            total = part[core, xh, p, m] + wp_recv[p, xh, m].astype(F32)
            wz_send[p, m] = (total + wx_recv[p, m].astype(F32)).astype(BF16)

        @pl.when(z % 2 == p)
        def _():
            wz_recv[z] = wz_send[p, z // 2]

        @pl.loop(0, pairs_of_levels)
        def _(j):
            m = (z // 2 + j) % pairs_of_levels

            @pl.when(2 * m + p != z)
            def _():
                w_level(p, m).start()

    w_part(0)
    w_pair_start(0)
    w_part(1)
    w_pair_start(1)
    qg[1].run()
    w_cross_start(0)
    qg[2].run()
    qg[3].run()
    w_cross_start(1)
    qg[0].finish()
    w_level_start(0)

    def final_pair(n):
        for column in pairs[n]:
            for u in range(2):
                h = 2 * column + u
                after = state[1, h]
                grad = dot(v_of(h), after, NT) + acc_k[:, head_cols(h)]
                kg_ref[:, head_cols(h)] = (factor * grad).astype(BF16)
                grad = dot(k_of(h), after) + acc_v[:, head_cols(h)]
                vg_ref[:, head_cols(h)] = (factor * grad).astype(BF16)

    for n in range(1, 3):
        qg[n].finish()
    for n in range(3):
        qg[n].wait()
        final_pair(n)
    w_level_start(1)
    qg[3].finish()
    qg[3].wait()
    final_pair(3)
    passed = [*own, *own_across, *past_up, *past_down, *partner_up.values(), *partner_down.values()]
    for copy in (*passed, *far_across.values(), down_across, up_across):
        copy.wait_send()

    for n, row in enumerate((up, down, far)):
        g_copy(n, row).wait_send()
    w_side.wait_send()
    w_share.wait_send()
    at_all().wait_send()
    kv.drain()
    for scan in qg:
        scan.drain()
    for p in range(2):
        w_pair(p).wait_send()
        w_cross(p).wait_send()
    w_levels().wait_recv()
    total = wz_recv[0].astype(F32)
    for j in range(1, levels):
        total = total + wz_recv[j].astype(F32)
    wg_ref[...] = total * grad_factor
    w_levels().wait_send()


def store(*refs):
    sems = refs[-1]
    copies = [pltpu.make_async_copy(refs[i], refs[4 + i], sems.at[i]) for i in range(4)]
    for copy in copies:
        copy.start()
    for copy in copies:
        copy.wait()


def body(queries, key_vectors, value_vectors, out_grad, out_weight):
    seq_devices = lax.axis_size("seq")
    group = lax.axis_size("fsdp")
    chips = seq_devices // 2
    _, tokens, width_all = queries.shape
    depth, width = out_weight.shape
    factor = 1.0 / math.sqrt(HEAD_DIM * tokens * seq_devices)
    grad_factor = 1.0 / math.sqrt(group * tokens * seq_devices)
    half = HEADS // 2
    out_rows = depth // seq_devices
    flat = (tokens, width_all)
    vmem = pl.BlockSpec(memory_space=pltpu.VMEM)
    levels = chips // 2
    pieces = (levels // 2, out_rows, width)
    blocks = pltpu.VMEM((group, tokens, width), BF16)
    square = (HEAD_DIM, HEAD_DIM)
    chunk = (4, 2)
    dma = pltpu.SemaphoreType.DMA
    shapes = (
        jax.ShapeDtypeStruct(flat, BF16),
        jax.ShapeDtypeStruct(flat, BF16),
        jax.ShapeDtypeStruct(flat, BF16),
        jax.ShapeDtypeStruct((out_rows, width), F32),
    )
    args = [x.reshape(flat) for x in (queries, key_vectors, value_vectors, out_grad)]
    args = [pltpu.with_memory_space_constraint(x, pltpu.HBM) for x in (*args, out_weight)]
    results = pl.pallas_call(
        functools.partial(kernel, chips, group // 2, factor, grad_factor),
        out_shape=shapes,
        in_specs=[pl.BlockSpec(memory_space=pltpu.HBM)] * 5,
        out_specs=(vmem,) * 4,
        scratch_shapes=[
            pltpu.VMEM(flat, BF16),
            pltpu.VMEM(flat, BF16),
            pltpu.VMEM(flat, BF16),
            pltpu.VMEM((2, depth, width), BF16),
            pltpu.VMEM((group, tokens, depth), BF16),
            blocks,
            pltpu.VMEM((3, 2, tokens, width), BF16),
            blocks,
            blocks,
            pltpu.VMEM((half,) + square, F32),
            pltpu.VMEM((half,) + square, F32),
            pltpu.VMEM((half,) + square, F32),
            pltpu.VMEM((4, chips, half * HEAD_DIM // chips, HEAD_DIM), BF16),
            pltpu.VMEM((half,) + square, BF16),
            pltpu.VMEM(chunk + square, F32),
            pltpu.VMEM(chunk + square, F32),
            pltpu.VMEM(chunk + square, F32),
            pltpu.VMEM((4, 4, chips, 2 * HEAD_DIM // chips, HEAD_DIM), BF16),
            pltpu.VMEM(chunk + square, BF16),
            pltpu.VMEM((2, HEADS) + square, BF16),
            pltpu.VMEM(flat, F32),
            pltpu.VMEM(flat, F32),
            pltpu.VMEM(flat, F32),
            pltpu.VMEM((2, 2, 2, levels // 2, out_rows, width), F32),
            pltpu.VMEM((2, 2) + pieces, BF16),
            pltpu.VMEM((2, 2) + pieces, BF16),
            pltpu.VMEM((2,) + pieces, BF16),
            pltpu.VMEM((2,) + pieces, BF16),
            pltpu.VMEM((2,) + pieces, BF16),
            pltpu.VMEM((levels, out_rows, width), BF16),
            dma((5,)),
            dma((8, 4)),
            dma((group, 4)),
            dma((3,)),
            dma((group // 2,)),
            dma((1,)),
            dma((1,)),
            dma((10,)),
            dma((10,)),
            dma((10,)),
            dma((10,)),
            dma((8,)),
            dma((8,)),
        ],
        compiler_params=pltpu.CompilerParams(
            collective_id=0, has_side_effects=True, vmem_limit_bytes=44 * 1024 * 1024
        ),
    )(*args)
    results = pl.pallas_call(
        store,
        out_shape=shapes,
        in_specs=[vmem] * 4,
        out_specs=(pl.BlockSpec(memory_space=pltpu.HBM),) * 4,
        scratch_shapes=[dma((4,))],
        compiler_params=pltpu.CompilerParams(vmem_limit_bytes=16 * 1024 * 1024),
    )(*results)
    whole = (1,) + flat
    return (
        results[0].reshape(whole),
        results[1].reshape(whole),
        results[2].reshape(whole),
        results[3],
    )


def solution(mesh):
    in_specs = (
        P("fsdp", "seq", None),
        P("fsdp", "seq", None),
        P("fsdp", "seq", None),
        P("fsdp", "seq", None),
        P(None, "fsdp"),
    )
    out_specs = (
        P("fsdp", "seq", None),
        P("fsdp", "seq", None),
        P("fsdp", "seq", None),
        P("seq", "fsdp"),
    )
    return jax.shard_map(body, mesh=mesh, in_specs=in_specs, out_specs=out_specs, check_vma=False)
```

```python
import functools
import math

import jax
import jax.numpy as jnp
from jax import lax
from jax.experimental import pallas as pl
from jax.experimental.pallas import tpu as pltpu
from jax.sharding import PartitionSpec as P

HEADS = 16
HEAD_DIM = 128
BLOCK = 128
MESH = pl.DeviceIdType.MESH
F32 = jnp.float32
BF16 = jnp.bfloat16
NT = (((1,), (1,)), ((), ()))
TN = (((0,), (0,)), ((), ()))


def dot(a, b, dims=(((1,), (0,)), ((), ()))):
    return lax.dot_general(a, b, dims, preferred_element_type=F32)


def head_cols(h):
    return pl.ds(pl.multiple_of(h * HEAD_DIM, HEAD_DIM), HEAD_DIM)


def kernel(
    chips,
    ring,
    factor,
    grad_factor,
    q_in,
    k_in,
    v_in,
    og_in,
    w_in,
    qg_ref,
    kg_ref,
    vg_ref,
    wg_ref,
    q_ref,
    k_ref,
    v_ref,
    w_all,
    og_all,
    gbuf,
    gsend,
    att_all,
    att_send,
    contrib0,
    xc_send0,
    xc_recv0,
    slices0,
    p_out0,
    contrib1,
    xc_send1,
    xc_recv1,
    slices1,
    p_out1,
    state,
    acc_a,
    acc_k,
    acc_v,
    part,
    wp_send,
    wp_recv,
    wx_send,
    wx_recv,
    wz_send,
    wz_recv,
    in_sem,
    ag_ss,
    ag_rs,
    g_ss,
    g_rs,
    at_ss,
    at_rs,
    x_ss,
    x_rs,
    a_ss,
    a_rs,
    w_ss,
    w_rs,
):
    s = lax.axis_index("seq")
    f = lax.axis_index("fsdp")
    group = 2 * ring
    half = HEADS // 2
    chip, core = s // 2, s % 2
    levels = chips // 2
    z, xh = chip // 2, chip % 2
    across = (2 * z + 1 - xh) * 2 + core
    mate = s + 1 - 2 * core
    yy, xl = f // 2, f % 2
    xp = f + 1 - 2 * xl
    up = ((yy + 1) % ring) * 2
    down = ((yy + ring - 1) % ring) * 2
    far = ((yy + 2) % ring) * 2
    ol = 1 - xl

    def remote(src, dst, ssem, rsem, dev):
        return pltpu.make_async_remote_copy(
            src_ref=src,
            dst_ref=dst,
            send_sem=ssem,
            recv_sem=rsem,
            device_id=dev,
            device_id_type=MESH,
        )

    load_k = pltpu.make_async_copy(k_in, k_ref, in_sem.at[0])
    load_v = pltpu.make_async_copy(v_in, v_ref, in_sem.at[1])
    load_og = pltpu.make_async_copy(og_in, og_all.at[yy], in_sem.at[2])
    load_w = pltpu.make_async_copy(w_in, w_all.at[xl], in_sem.at[3])
    load_q = pltpu.make_async_copy(q_in, q_ref, in_sem.at[4])
    for load in (load_k, load_v, load_og, load_w, load_q):
        load.start()
    barrier = pltpu.get_barrier_semaphore()

    @pl.loop(1, ring)
    def _(j):
        row = (2 * yy + 2 * j) % group
        pl.semaphore_signal(barrier, inc=1, device_id=(s, row + xl), device_id_type=MESH)

    @pl.loop(1, chips)
    def _(j):
        other = ((chip + j) % chips) * 2 + core
        pl.semaphore_signal(barrier, inc=1, device_id=(other, f), device_id_type=MESH)

    pl.semaphore_signal(barrier, inc=1, device_id=(mate, f), device_id_type=MESH)
    pl.semaphore_signal(barrier, inc=1, device_id=(across, xp), device_id_type=MESH)
    pl.semaphore_signal(barrier, inc=1, device_id=(s, xp), device_id_type=MESH)
    pl.semaphore_wait(barrier, ring - 1 + chips - 1 + 3)

    def quarter_view(ref, part_at):
        return ref.at[pl.ds(part_at * (BLOCK // 4), BLOCK // 4)]

    def ag_own(n, part_at, dev):
        return remote(
            quarter_view(og_in, part_at), quarter_view(og_all.at[yy], part_at),
            ag_ss.at[n, part_at], ag_rs.at[yy, part_at], (s, dev),
        )

    def ag_pass(n, slot, part_at, dev):
        view = quarter_view(og_all.at[slot], part_at)
        return remote(view, view, ag_ss.at[n, part_at], ag_rs.at[slot, part_at], (s, dev))

    def ag_wait(slot, *parts_at):
        for part_at in parts_at:
            ag_pass(0, slot, part_at, xp).wait_recv()

    own = [ag_own(0, p, up + xl) for p in range(4)] + [ag_own(1, p, down + xl) for p in (3, 2, 1, 0)]
    past_up = [ag_pass(2, down // 2, p, up + xl) for p in (0, 1)]
    past_down = [ag_pass(2, up // 2, p, down + xl) for p in (3, 2)]

    w_part = w_in.shape[0] // 2
    w_rows_here = pl.ds(core * w_part, w_part)
    w_rows_mate = pl.ds((1 - core) * w_part, w_part)
    w_side = remote(
        w_in.at[w_rows_here], w_all.at[xl, w_rows_here], w_ss.at[9], w_rs.at[9], (across, xp)
    )
    w_got = w_all.at[1 - xl, w_rows_here]
    w_share = remote(w_got, w_got, w_ss.at[10], w_rs.at[10], (mate, f))

    w_side.start()
    for p in range(4):
        own[p].start()
        own[4 + p].start()

    def q_of(h):
        return q_ref[:, head_cols(h)]

    def k_of(h):
        return k_ref[:, head_cols(h)]

    def v_of(h):
        return v_ref[:, head_cols(h)]

    def g_of(h):
        return gbuf[h // 2, :, pl.ds(pl.multiple_of((h % 2) * HEAD_DIM, HEAD_DIM), HEAD_DIM)]

    def a2a_copy(src, dst, n, there):
        return remote(src, dst, a_ss.at[n], a_rs.at[n], (there * 2 + core, f))

    def a2a_start(src, dst, n):
        @pl.loop(1, chips)
        def _(j):
            there = (chip + j) % chips
            a2a_copy(src.at[there], dst.at[chip], n, there).start()

    def a2a_all(src, dst, n):
        every = pl.ds(0, chips - 1)
        return remote(src.at[every], dst.at[every], a_ss.at[n], a_rs.at[n], (mate, f))

    def a2a_wait(src, dst, n):
        a2a_all(src, dst, n).wait_recv()

    def a2a_drain(src, dst, n):
        a2a_all(src, dst, n).wait_send()

    class Scan:
        def __init__(self, at, b, reverse, mine, other, left, right, bufs):
            self.at, self.b, self.reverse = at, b, reverse
            self.mine, self.other, self.left, self.right = mine, other, left, right
            self.contrib, self.xc_send, self.xc_recv, slices, self.p_out = bufs
            self.a_send, self.a_recv, self.r_send, self.r_recv = [slices.at[i] for i in range(4)]
            self.heads = self.contrib.shape[0]
            self.rows = self.heads * HEAD_DIM // chips

        def pair(self):
            return remote(
                self.xc_send, self.xc_recv, x_ss.at[2 * self.at], x_rs.at[2 * self.at], (mate, f)
            )

        def place(self, j):
            row = pl.multiple_of((j * self.rows) % HEAD_DIM, self.rows)
            return j * self.rows // HEAD_DIM, pl.ds(row, self.rows)

        def start(self):
            @pl.loop(0, self.heads // 2)
            def _(i):
                for u in range(2):
                    h = self.other + 2 * i + u
                    self.xc_send[2 * i + u] = dot(self.left(h), self.right(h), TN)

            self.pair().start()

            @pl.loop(0, self.heads // 2)
            def _(i):
                for u in range(2):
                    h = self.mine + 2 * i + u
                    self.contrib[2 * i + u] = dot(self.left(h), self.right(h), TN)

        def spread(self):
            self.pair().wait_recv()

            @pl.loop(0, chips)
            def _(j):
                head, rows = self.place(j)
                self.a_send[j] = (self.contrib[head, rows] + self.xc_recv[head, rows]).astype(BF16)

            self.a_recv[chip] = self.a_send[chip]
            a2a_start(self.a_send, self.a_recv, 2 * self.at)

        def run(self):
            a2a_wait(self.a_send, self.a_recv, 2 * self.at)
            total = jnp.zeros((self.rows, HEAD_DIM), F32)
            for j in range(chips):
                at = chips - 1 - j if self.reverse else j
                self.r_send[at] = total.astype(BF16)
                total = total + self.a_recv[at].astype(F32)
            self.r_recv[chip] = self.r_send[chip]
            a2a_start(self.r_send, self.r_recv, 2 * self.at + 1)

        def back(self):
            heads = pl.ds(self.mine, self.heads)
            return remote(
                self.p_out, state.at[self.b, heads],
                x_ss.at[2 * self.at + 1], x_rs.at[2 * self.at + 1], (mate, f),
            )

        def finish(self):
            a2a_wait(self.r_send, self.r_recv, 2 * self.at + 1)
            first = core == (1 if self.reverse else 0)

            @pl.loop(0, chips)
            def _(j):
                head, rows = self.place(j)
                carried = self.r_recv[j].astype(F32)
                mine, theirs = self.contrib[head, rows], self.xc_recv[head, rows]
                self.p_out[head, rows] = (carried + jnp.where(first, mine, 0.0)).astype(BF16)
                state[self.b, self.mine + head, rows] = (
                    carried + jnp.where(first, 0.0, theirs)
                ).astype(BF16)

            self.back().start()

        def wait(self):
            heads = pl.ds(self.other, self.heads)
            remote(
                self.p_out, state.at[self.b, heads],
                x_ss.at[2 * self.at + 1], x_rs.at[2 * self.at + 1], (mate, f),
            ).wait_recv()

        def drain(self):
            self.pair().wait_send()
            self.back().wait_send()
            a2a_drain(self.a_send, self.a_recv, 2 * self.at)
            a2a_drain(self.r_send, self.r_recv, 2 * self.at + 1)

    kv = Scan(
        0, 0, False, core * half, (1 - core) * half, k_of, v_of,
        (contrib0, xc_send0, xc_recv0, slices0, p_out0),
    )
    pairs = tuple((row, row + 1) for row in (2 * yy, up, down, far))
    qg = []
    for n, (first, second) in enumerate(pairs):
        mine = 2 * (first + core * (second - first))
        other = 2 * (second + core * (first - second))
        bufs = tuple(ref.at[n] for ref in (contrib1, xc_send1, xc_recv1, slices1, p_out1))
        qg.append(Scan(1 + n, 1, True, mine, other, q_of, g_of, bufs))

    load_k.wait()
    load_v.wait()
    kv.start()
    kv.spread()

    def g_copy(n, row):
        to = gbuf.at[pl.ds(2 * yy, 2)]
        return remote(gsend.at[n], to, g_ss.at[n], g_rs.at[yy], (s, row + xl))

    def g_make(n, row):
        for c in range(2):
            gsend[n, c] = dot(og_all[row // 2], w_all[c]).astype(BF16)

    def g_wait(row):
        at = gbuf.at[pl.ds(row, 2)]
        remote(gsend.at[0], at, g_ss.at[0], g_rs.at[row // 2], (s, row + xl)).wait_recv()

    row_index = lax.broadcasted_iota(jnp.int32, (BLOCK, BLOCK), 0)
    col_index = lax.broadcasted_iota(jnp.int32, (BLOCK, BLOCK), 1)
    lower = row_index >= col_index
    upper = row_index <= col_index
    load_q.wait()

    @pl.loop(0, HEADS // 2)
    def _(i):
        for u in range(2):
            h = 2 * i + u
            scores = jnp.where(lower, dot(q_of(h), k_of(h), NT), 0.0).astype(BF16)
            acc_a[:, head_cols(h)] = dot(scores, v_of(h))

    for n in range(2):
        ag_wait(down // 2, n)
        past_up[n].start()
        ag_wait(up // 2, 3 - n)
        past_down[n].start()
    kv.run()
    remote(
        w_in.at[w_rows_here], w_got, w_ss.at[9], w_rs.at[9], (across, xp)
    ).wait_recv()
    w_share.start()
    load_og.wait()
    load_w.wait()
    ag_wait(down // 2, 2, 3)
    ag_wait(up // 2, 1, 0)
    w_theirs = w_all.at[1 - xl, w_rows_mate]
    remote(w_theirs, w_theirs, w_ss.at[10], w_rs.at[10], (mate, f)).wait_recv()
    for c in range(2):
        gbuf[2 * yy + c] = dot(og_all[yy], w_all[c]).astype(BF16)
    g_make(0, up)
    g_copy(0, up).start()
    g_make(1, down)
    g_copy(1, down).start()

    def local_grads(h):
        q, k, v, g = q_of(h), k_of(h), v_of(h), g_of(h)
        mixing = jnp.where(lower, dot(g, v, NT), 0.0).astype(BF16)
        grad = dot(mixing, k) + dot(g, state[0, h], NT)
        qg_ref[:, head_cols(h)] = (factor * grad).astype(BF16)
        mixing_t = jnp.where(upper, dot(v, g, NT), 0.0).astype(BF16)
        acc_k[:, head_cols(h)] = dot(mixing_t, q)
        scores_t = jnp.where(upper, dot(k, q, NT), 0.0).astype(BF16)
        acc_v[:, head_cols(h)] = dot(scores_t, g)

    def local_pair(n):
        for column in pairs[n]:
            for u in range(2):
                local_grads(2 * column + u)

    def at_copy(row):
        return remote(
            att_send.at[row // 2], att_all.at[yy], at_ss.at[0], at_rs.at[0], (s, row + xl)
        )

    def at_every():
        some = pl.ds(0, ring - 1)
        return remote(att_send.at[some], att_all.at[some], at_ss.at[0], at_rs.at[0], (mate, f))

    qg[0].start()
    qg[0].spread()
    ag_wait(far // 2, 0, 3, 1, 2)
    g_make(2, far)
    g_copy(2, far).start()
    kv.finish()
    kv.wait()
    @pl.loop(0, ring)
    def _(i):
        for u in range(HEADS // ring):
            h = i * (HEADS // ring) + u
            attended = dot(q_of(h), state[0, h]) + acc_a[:, head_cols(h)]
            att_send[i, :, u * HEAD_DIM:(u + 1) * HEAD_DIM] = (factor * attended).astype(BF16)

    att_all[yy] = att_send[yy]
    for row in (up, down, far):
        at_copy(row).start()
    local_pair(0)
    g_wait(up)
    qg[1].start()
    qg[1].spread()
    g_wait(down)
    qg[2].start()
    qg[2].spread()
    local_pair(1)
    qg[0].run()
    g_wait(far)
    qg[3].start()
    qg[3].spread()

    depth, width = w_in.shape
    out_rows = wg_ref.shape[0]
    step = 256
    rows_all = ring * BLOCK
    pairs_of_levels = levels // 2

    def w_part(p):
        @pl.loop(0, pairs_of_levels)
        def _(m):
            cols = pl.ds(pl.multiple_of((2 * m + p) * step, step), step)
            left = og_all[:, :, cols].reshape(rows_all, step)
            piece = dot(left, att_all[...].reshape(rows_all, 2 * width), TN)
            for n in range(2):
                for c in range(2):
                    base = (2 * n + c) * out_rows
                    for x in range(2):
                        rows = piece[base:base + out_rows, x * width:(x + 1) * width]
                        part[c, n, x, p, m] = rows

    def w_pair(p):
        return remote(wp_send.at[p], wp_recv.at[p], w_ss.at[p], w_rs.at[p], (mate, f))

    ring_x = ((xh, ol), (1 - xh, xl), (1 - xh, ol))

    def w_cross(p, n):
        xh_there, xl_there = ring_x[n]
        to = ((2 * z + xh_there) * 2 + core, 2 * yy + xl_there)
        at = 2 + 3 * p + n
        return remote(wx_send.at[p, n], wx_recv.at[p, n], w_ss.at[at], w_rs.at[at], to)

    def w_level(p, m):
        to = (2 * (2 * m + p) + xh) * 2 + core
        return remote(wz_send.at[p, m], wz_recv.at[z], w_ss.at[8], w_rs.at[8], (to, f))

    def w_levels():
        every = wz_recv.at[pl.ds(0, levels - 1)]
        return remote(every, every, w_ss.at[8], w_rs.at[8], (mate, f))

    def w_pair_start(p):
        @pl.loop(0, pairs_of_levels)
        def _(m):
            for n in range(2):
                for x in range(2):
                    wp_send[p, n, x, m] = part[1 - core, n, x, p, m].astype(BF16)

        w_pair(p).start()

    def w_cross_start(p):
        w_pair(p).wait_recv()
        for n in (1, 0, 2):
            xh_there, xl_there = ring_x[n]

            @pl.loop(0, pairs_of_levels)
            def _(m):
                total = part[core, xh_there, xl_there, p, m]
                total = total + wp_recv[p, xh_there, xl_there, m].astype(F32)
                wx_send[p, n, m] = total.astype(BF16)

            w_cross(p, n).start()

    def w_level_start(p):
        for n in range(3):
            w_cross(p, n).wait_recv()

        @pl.loop(0, pairs_of_levels)
        def _(m):
            total = part[core, xh, xl, p, m] + wp_recv[p, xh, xl, m].astype(F32)
            for n in range(3):
                total = total + wx_recv[p, n, m].astype(F32)
            wz_send[p, m] = total.astype(BF16)

        @pl.when(z % 2 == p)
        def _():
            wz_recv[z] = wz_send[p, z // 2]

        @pl.loop(0, pairs_of_levels)
        def _(j):
            m = (z // 2 + j) % pairs_of_levels

            @pl.when(2 * m + p != z)
            def _():
                w_level(p, m).start()

    at_every().wait_recv()
    w_part(0)
    w_pair_start(0)
    w_part(1)
    w_pair_start(1)
    qg[1].run()
    w_cross_start(0)
    qg[2].run()
    w_cross_start(1)
    qg[3].run()
    local_pair(2)
    local_pair(3)
    qg[0].finish()

    def final_pair(n):
        for column in pairs[n]:
            for u in range(2):
                h = 2 * column + u
                after = state[1, h]
                grad = dot(v_of(h), after, NT) + acc_k[:, head_cols(h)]
                kg_ref[:, head_cols(h)] = (factor * grad).astype(BF16)
                grad = dot(k_of(h), after) + acc_v[:, head_cols(h)]
                vg_ref[:, head_cols(h)] = (factor * grad).astype(BF16)

    for n in range(1, 3):
        qg[n].finish()
    for n in range(3):
        qg[n].wait()
        final_pair(n)
    w_level_start(0)
    qg[3].finish()
    w_level_start(1)
    qg[3].wait()
    final_pair(3)
    for copy in (*own, *past_up, *past_down):
        copy.wait_send()

    for n, row in enumerate((up, down, far)):
        g_copy(n, row).wait_send()
    w_side.wait_send()
    w_share.wait_send()
    at_every().wait_send()
    kv.drain()
    for scan in qg:
        scan.drain()
    for p in range(2):
        w_pair(p).wait_send()
        for n in range(3):
            w_cross(p, n).wait_send()
    w_levels().wait_recv()
    total = wz_recv[0].astype(F32)
    for j in range(1, levels):
        total = total + wz_recv[j].astype(F32)
    wg_ref[...] = total * grad_factor
    w_levels().wait_send()


def store(*refs):
    sems = refs[-1]
    copies = [pltpu.make_async_copy(refs[i], refs[4 + i], sems.at[i]) for i in range(4)]
    for copy in copies:
        copy.start()
    for copy in copies:
        copy.wait()


def body(queries, key_vectors, value_vectors, out_grad, out_weight):
    seq_devices = lax.axis_size("seq")
    group = lax.axis_size("fsdp")
    chips = seq_devices // 2
    _, tokens, width_all = queries.shape
    depth, width = out_weight.shape
    factor = 1.0 / math.sqrt(HEAD_DIM * tokens * seq_devices)
    grad_factor = 1.0 / math.sqrt(group * tokens * seq_devices)
    half = HEADS // 2
    out_rows = depth // seq_devices
    flat = (tokens, width_all)
    vmem = pl.BlockSpec(memory_space=pltpu.VMEM)
    levels = chips // 2
    ring = group // 2
    pieces = (levels // 2, out_rows, width)
    blocks = pltpu.VMEM((group, tokens, width), BF16)
    square = (HEAD_DIM, HEAD_DIM)
    chunk = (4, 2)
    dma = pltpu.SemaphoreType.DMA
    shapes = (
        jax.ShapeDtypeStruct(flat, BF16),
        jax.ShapeDtypeStruct(flat, BF16),
        jax.ShapeDtypeStruct(flat, BF16),
        jax.ShapeDtypeStruct((out_rows, width), F32),
    )
    args = [x.reshape(flat) for x in (queries, key_vectors, value_vectors, out_grad)]
    args = [pltpu.with_memory_space_constraint(x, pltpu.HBM) for x in (*args, out_weight)]
    results = pl.pallas_call(
        functools.partial(kernel, chips, group // 2, factor, grad_factor),
        out_shape=shapes,
        in_specs=[pl.BlockSpec(memory_space=pltpu.HBM)] * 5,
        out_specs=(vmem,) * 4,
        scratch_shapes=[
            pltpu.VMEM(flat, BF16),
            pltpu.VMEM(flat, BF16),
            pltpu.VMEM(flat, BF16),
            pltpu.VMEM((2, depth, width), BF16),
            pltpu.VMEM((ring, tokens, depth), BF16),
            blocks,
            pltpu.VMEM((3, 2, tokens, width), BF16),
            pltpu.VMEM((ring, tokens, 2 * width), BF16),
            pltpu.VMEM((ring, tokens, 2 * width), BF16),
            pltpu.VMEM((half,) + square, F32),
            pltpu.VMEM((half,) + square, F32),
            pltpu.VMEM((half,) + square, F32),
            pltpu.VMEM((4, chips, half * HEAD_DIM // chips, HEAD_DIM), BF16),
            pltpu.VMEM((half,) + square, BF16),
            pltpu.VMEM(chunk + square, F32),
            pltpu.VMEM(chunk + square, F32),
            pltpu.VMEM(chunk + square, F32),
            pltpu.VMEM((4, 4, chips, 2 * HEAD_DIM // chips, HEAD_DIM), BF16),
            pltpu.VMEM(chunk + square, BF16),
            pltpu.VMEM((2, HEADS) + square, BF16),
            pltpu.VMEM(flat, F32),
            pltpu.VMEM(flat, F32),
            pltpu.VMEM(flat, F32),
            pltpu.VMEM((2, 2, 2, 2, levels // 2, out_rows, width), F32),
            pltpu.VMEM((2, 2, 2) + pieces, BF16),
            pltpu.VMEM((2, 2, 2) + pieces, BF16),
            pltpu.VMEM((2, 3) + pieces, BF16),
            pltpu.VMEM((2, 3) + pieces, BF16),
            pltpu.VMEM((2,) + pieces, BF16),
            pltpu.VMEM((levels, out_rows, width), BF16),
            dma((5,)),
            dma((3, 4)),
            dma((ring, 4)),
            dma((3,)),
            dma((ring,)),
            dma((1,)),
            dma((1,)),
            dma((10,)),
            dma((10,)),
            dma((10,)),
            dma((10,)),
            dma((11,)),
            dma((11,)),
        ],
        compiler_params=pltpu.CompilerParams(
            collective_id=0, has_side_effects=True, vmem_limit_bytes=44 * 1024 * 1024
        ),
    )(*args)
    results = pl.pallas_call(
        store,
        out_shape=shapes,
        in_specs=[vmem] * 4,
        out_specs=(pl.BlockSpec(memory_space=pltpu.HBM),) * 4,
        scratch_shapes=[dma((4,))],
        compiler_params=pltpu.CompilerParams(vmem_limit_bytes=16 * 1024 * 1024),
    )(*results)
    whole = (1,) + flat
    return (
        results[0].reshape(whole),
        results[1].reshape(whole),
        results[2].reshape(whole),
        results[3],
    )


def solution(mesh):
    in_specs = (
        P("fsdp", "seq", None),
        P("fsdp", "seq", None),
        P("fsdp", "seq", None),
        P("fsdp", "seq", None),
        P(None, "fsdp"),
    )
    out_specs = (
        P("fsdp", "seq", None),
        P("fsdp", "seq", None),
        P("fsdp", "seq", None),
        P("seq", "fsdp"),
    )
    return jax.shard_map(body, mesh=mesh, in_specs=in_specs, out_specs=out_specs, check_vma=False)
```

```python
import functools
import math

import jax
import jax.numpy as jnp
from jax import lax
from jax.experimental import pallas as pl
from jax.experimental.pallas import tpu as pltpu
from jax.sharding import PartitionSpec as P

HEADS = 16
HEAD_DIM = 128
BLOCK = 128
PARTS = 4
MESH = pl.DeviceIdType.MESH
F32 = jnp.float32
BF16 = jnp.bfloat16
NT = (((1,), (1,)), ((), ()))
TN = (((0,), (0,)), ((), ()))


def dot(a, b, dims=(((1,), (0,)), ((), ()))):
    return lax.dot_general(a, b, dims, preferred_element_type=F32)


def head_cols(h):
    return pl.ds(pl.multiple_of(h * HEAD_DIM, HEAD_DIM), HEAD_DIM)


def kernel(
    chips,
    ring,
    factor,
    grad_factor,
    q_in,
    k_in,
    v_in,
    og_in,
    w_in,
    qg_ref,
    kg_ref,
    vg_ref,
    wg_ref,
    q_ref,
    k_ref,
    v_ref,
    w_all,
    og_all,
    gbuf,
    gsend,
    att_all,
    att_send,
    contrib0,
    xc_send0,
    xc_recv0,
    slices0,
    p_out0,
    contrib1,
    xc_send1,
    xc_recv1,
    slices1,
    p_out1,
    state,
    acc_a,
    acc_k,
    acc_v,
    part,
    wp_send,
    wp_recv,
    wx_send,
    wx_recv,
    wz_send,
    wz_recv,
    in_sem,
    ag_ss,
    ag_rs,
    g_ss,
    g_rs,
    at_ss,
    at_rs,
    x_ss,
    x_rs,
    a_ss,
    a_rs,
    w_ss,
    w_rs,
):
    s = lax.axis_index("seq")
    f = lax.axis_index("fsdp")
    group = 2 * ring
    half = HEADS // 2
    chip, core = s // 2, s % 2
    levels = chips // 2
    z, xh = chip // 2, chip % 2
    across = (2 * z + 1 - xh) * 2 + core
    mate = s + 1 - 2 * core
    yy, xl = f // 2, f % 2
    xp = f + 1 - 2 * xl
    up = ((yy + 1) % ring) * 2
    down = ((yy + ring - 1) % ring) * 2
    far = ((yy + 2) % ring) * 2
    ol = 1 - xl

    def remote(src, dst, ssem, rsem, dev):
        return pltpu.make_async_remote_copy(
            src_ref=src,
            dst_ref=dst,
            send_sem=ssem,
            recv_sem=rsem,
            device_id=dev,
            device_id_type=MESH,
        )

    load_k = pltpu.make_async_copy(k_in, k_ref, in_sem.at[0])
    load_v = pltpu.make_async_copy(v_in, v_ref, in_sem.at[1])
    load_og = pltpu.make_async_copy(og_in, og_all.at[yy], in_sem.at[2])
    load_w = pltpu.make_async_copy(w_in, w_all.at[xl], in_sem.at[3])
    load_q = pltpu.make_async_copy(q_in, q_ref, in_sem.at[4])
    for load in (load_k, load_v, load_og, load_w, load_q):
        load.start()
    barrier = pltpu.get_barrier_semaphore()

    @pl.loop(1, ring)
    def _(j):
        row = (2 * yy + 2 * j) % group
        pl.semaphore_signal(barrier, inc=1, device_id=(s, row + xl), device_id_type=MESH)

    @pl.loop(1, chips)
    def _(j):
        other = ((chip + j) % chips) * 2 + core
        pl.semaphore_signal(barrier, inc=1, device_id=(other, f), device_id_type=MESH)

    pl.semaphore_signal(barrier, inc=1, device_id=(mate, f), device_id_type=MESH)
    pl.semaphore_signal(barrier, inc=1, device_id=(across, xp), device_id_type=MESH)
    pl.semaphore_signal(barrier, inc=1, device_id=(s, xp), device_id_type=MESH)
    pl.semaphore_wait(barrier, ring - 1 + chips - 1 + 3)

    def quarter_view(ref, part_at):
        return ref.at[pl.ds(part_at * (BLOCK // 4), BLOCK // 4)]

    def ag_own(n, part_at, dev):
        return remote(
            quarter_view(og_in, part_at), quarter_view(og_all.at[yy], part_at),
            ag_ss.at[n, part_at], ag_rs.at[yy, part_at], (s, dev),
        )

    def ag_pass(n, slot, part_at, dev):
        view = quarter_view(og_all.at[slot], part_at)
        return remote(view, view, ag_ss.at[n, part_at], ag_rs.at[slot, part_at], (s, dev))

    def ag_wait(slot, *parts_at):
        for part_at in parts_at:
            ag_pass(0, slot, part_at, xp).wait_recv()

    own = [ag_own(0, p, up + xl) for p in range(4)] + [ag_own(1, p, down + xl) for p in (3, 2, 1, 0)]
    past_up = [ag_pass(2, down // 2, p, up + xl) for p in (0, 1)]
    past_down = [ag_pass(2, up // 2, p, down + xl) for p in (3, 2)]

    w_part = w_in.shape[0] // 2
    w_rows_here = pl.ds(core * w_part, w_part)
    w_rows_mate = pl.ds((1 - core) * w_part, w_part)
    w_side = remote(
        w_in.at[w_rows_here], w_all.at[xl, w_rows_here], w_ss.at[4 * PARTS + 1], w_rs.at[4 * PARTS + 1], (across, xp)
    )
    w_got = w_all.at[1 - xl, w_rows_here]
    w_share = remote(w_got, w_got, w_ss.at[4 * PARTS + 2], w_rs.at[4 * PARTS + 2], (mate, f))

    w_side.start()
    for p in range(4):
        own[p].start()
        own[4 + p].start()

    def q_of(h):
        return q_ref[:, head_cols(h)]

    def k_of(h):
        return k_ref[:, head_cols(h)]

    def v_of(h):
        return v_ref[:, head_cols(h)]

    def g_of(h):
        return gbuf[h // 2, :, pl.ds(pl.multiple_of((h % 2) * HEAD_DIM, HEAD_DIM), HEAD_DIM)]

    def a2a_copy(src, dst, n, there):
        return remote(src, dst, a_ss.at[n], a_rs.at[n], (there * 2 + core, f))

    def a2a_start(src, dst, n):
        @pl.loop(1, chips)
        def _(j):
            there = (chip + j) % chips
            a2a_copy(src.at[there], dst.at[chip], n, there).start()

    def a2a_all(src, dst, n):
        every = pl.ds(0, chips - 1)
        return remote(src.at[every], dst.at[every], a_ss.at[n], a_rs.at[n], (mate, f))

    def a2a_wait(src, dst, n):
        a2a_all(src, dst, n).wait_recv()

    def a2a_drain(src, dst, n):
        a2a_all(src, dst, n).wait_send()

    class Scan:
        def __init__(self, at, b, reverse, mine, other, left, right, bufs):
            self.at, self.b, self.reverse = at, b, reverse
            self.mine, self.other, self.left, self.right = mine, other, left, right
            self.contrib, self.xc_send, self.xc_recv, slices, self.p_out = bufs
            self.a_send, self.a_recv, self.r_send, self.r_recv = [slices.at[i] for i in range(4)]
            self.heads = self.contrib.shape[0]
            self.rows = self.heads * HEAD_DIM // chips

        def pair(self):
            return remote(
                self.xc_send, self.xc_recv, x_ss.at[2 * self.at], x_rs.at[2 * self.at], (mate, f)
            )

        def place(self, j):
            row = pl.multiple_of((j * self.rows) % HEAD_DIM, self.rows)
            return j * self.rows // HEAD_DIM, pl.ds(row, self.rows)

        def start(self):
            @pl.loop(0, self.heads // 2)
            def _(i):
                for u in range(2):
                    h = self.other + 2 * i + u
                    self.xc_send[2 * i + u] = dot(self.left(h), self.right(h), TN)

            self.pair().start()

            @pl.loop(0, self.heads // 2)
            def _(i):
                for u in range(2):
                    h = self.mine + 2 * i + u
                    self.contrib[2 * i + u] = dot(self.left(h), self.right(h), TN)

        def spread(self):
            self.pair().wait_recv()

            @pl.loop(0, chips)
            def _(j):
                head, rows = self.place(j)
                self.a_send[j] = (self.contrib[head, rows] + self.xc_recv[head, rows]).astype(BF16)

            self.a_recv[chip] = self.a_send[chip]
            a2a_start(self.a_send, self.a_recv, 2 * self.at)

        def run(self):
            a2a_wait(self.a_send, self.a_recv, 2 * self.at)
            total = jnp.zeros((self.rows, HEAD_DIM), F32)
            for j in range(chips):
                at = chips - 1 - j if self.reverse else j
                self.r_send[at] = total.astype(BF16)
                total = total + self.a_recv[at].astype(F32)
            self.r_recv[chip] = self.r_send[chip]
            a2a_start(self.r_send, self.r_recv, 2 * self.at + 1)

        def back(self):
            heads = pl.ds(self.mine, self.heads)
            return remote(
                self.p_out, state.at[self.b, heads],
                x_ss.at[2 * self.at + 1], x_rs.at[2 * self.at + 1], (mate, f),
            )

        def finish(self):
            a2a_wait(self.r_send, self.r_recv, 2 * self.at + 1)
            first = core == (1 if self.reverse else 0)

            @pl.loop(0, chips)
            def _(j):
                head, rows = self.place(j)
                carried = self.r_recv[j].astype(F32)
                mine, theirs = self.contrib[head, rows], self.xc_recv[head, rows]
                self.p_out[head, rows] = (carried + jnp.where(first, mine, 0.0)).astype(BF16)
                state[self.b, self.mine + head, rows] = (
                    carried + jnp.where(first, 0.0, theirs)
                ).astype(BF16)

            self.back().start()

        def wait(self):
            heads = pl.ds(self.other, self.heads)
            remote(
                self.p_out, state.at[self.b, heads],
                x_ss.at[2 * self.at + 1], x_rs.at[2 * self.at + 1], (mate, f),
            ).wait_recv()

        def drain(self):
            self.pair().wait_send()
            self.back().wait_send()
            a2a_drain(self.a_send, self.a_recv, 2 * self.at)
            a2a_drain(self.r_send, self.r_recv, 2 * self.at + 1)

    kv = Scan(
        0, 0, False, core * half, (1 - core) * half, k_of, v_of,
        (contrib0, xc_send0, xc_recv0, slices0, p_out0),
    )
    pairs = tuple((row, row + 1) for row in (2 * yy, up, down, far))
    qg = []
    for n, (first, second) in enumerate(pairs):
        mine = 2 * (first + core * (second - first))
        other = 2 * (second + core * (first - second))
        bufs = tuple(ref.at[n] for ref in (contrib1, xc_send1, xc_recv1, slices1, p_out1))
        qg.append(Scan(1 + n, 1, True, mine, other, q_of, g_of, bufs))

    load_k.wait()
    load_v.wait()
    kv.start()
    kv.spread()

    def g_copy(n, row):
        to = gbuf.at[pl.ds(2 * yy, 2)]
        return remote(gsend.at[n], to, g_ss.at[n], g_rs.at[yy], (s, row + xl))

    def g_make(n, row):
        for c in range(2):
            gsend[n, c] = dot(og_all[row // 2], w_all[c]).astype(BF16)

    def g_wait(row):
        at = gbuf.at[pl.ds(row, 2)]
        remote(gsend.at[0], at, g_ss.at[0], g_rs.at[row // 2], (s, row + xl)).wait_recv()

    row_index = lax.broadcasted_iota(jnp.int32, (BLOCK, BLOCK), 0)
    col_index = lax.broadcasted_iota(jnp.int32, (BLOCK, BLOCK), 1)
    lower = row_index >= col_index
    upper = row_index <= col_index
    load_q.wait()

    @pl.loop(0, HEADS // 2)
    def _(i):
        for u in range(2):
            h = 2 * i + u
            scores = jnp.where(lower, dot(q_of(h), k_of(h), NT), 0.0).astype(BF16)
            acc_a[:, head_cols(h)] = dot(scores, v_of(h))

    for n in range(2):
        ag_wait(down // 2, n)
        past_up[n].start()
        ag_wait(up // 2, 3 - n)
        past_down[n].start()
    kv.run()
    remote(
        w_in.at[w_rows_here], w_got, w_ss.at[4 * PARTS + 1], w_rs.at[4 * PARTS + 1], (across, xp)
    ).wait_recv()
    w_share.start()
    load_og.wait()
    load_w.wait()
    ag_wait(down // 2, 2, 3)
    ag_wait(up // 2, 1, 0)
    w_theirs = w_all.at[1 - xl, w_rows_mate]
    remote(w_theirs, w_theirs, w_ss.at[4 * PARTS + 2], w_rs.at[4 * PARTS + 2], (mate, f)).wait_recv()
    for c in range(2):
        gbuf[2 * yy + c] = dot(og_all[yy], w_all[c]).astype(BF16)
    g_make(0, up)
    g_copy(0, up).start()
    g_make(1, down)
    g_copy(1, down).start()

    def local_grads(h):
        q, k, v, g = q_of(h), k_of(h), v_of(h), g_of(h)
        mixing = jnp.where(lower, dot(g, v, NT), 0.0).astype(BF16)
        grad = dot(mixing, k) + dot(g, state[0, h], NT)
        qg_ref[:, head_cols(h)] = (factor * grad).astype(BF16)
        mixing_t = jnp.where(upper, dot(v, g, NT), 0.0).astype(BF16)
        acc_k[:, head_cols(h)] = dot(mixing_t, q)
        scores_t = jnp.where(upper, dot(k, q, NT), 0.0).astype(BF16)
        acc_v[:, head_cols(h)] = dot(scores_t, g)

    def local_pair(n):
        for column in pairs[n]:
            for u in range(2):
                local_grads(2 * column + u)

    def at_copy(row):
        return remote(
            att_send.at[row // 2], att_all.at[yy], at_ss.at[0], at_rs.at[0], (s, row + xl)
        )

    def at_every():
        some = pl.ds(0, ring - 1)
        return remote(att_send.at[some], att_all.at[some], at_ss.at[0], at_rs.at[0], (mate, f))

    qg[0].start()
    qg[0].spread()
    ag_wait(far // 2, 0, 3, 1, 2)
    g_make(2, far)
    g_copy(2, far).start()
    kv.finish()
    kv.wait()
    @pl.loop(0, ring)
    def _(i):
        for u in range(HEADS // ring):
            h = i * (HEADS // ring) + u
            attended = dot(q_of(h), state[0, h]) + acc_a[:, head_cols(h)]
            att_send[i, :, u * HEAD_DIM:(u + 1) * HEAD_DIM] = (factor * attended).astype(BF16)

    att_all[yy] = att_send[yy]
    for row in (up, down, far):
        at_copy(row).start()
    local_pair(0)
    g_wait(up)
    qg[1].start()
    qg[1].spread()
    g_wait(down)
    qg[2].start()
    qg[2].spread()
    local_pair(1)
    qg[0].run()
    g_wait(far)
    qg[3].start()
    qg[3].spread()

    depth, width = w_in.shape
    out_rows = wg_ref.shape[0]
    step = 256
    rows_all = ring * BLOCK
    levels_of_part = levels // PARTS

    def w_part(p):
        @pl.loop(0, levels_of_part)
        def _(m):
            cols = pl.ds(pl.multiple_of((PARTS * m + p) * step, step), step)
            left = og_all[:, :, cols].reshape(rows_all, step)
            piece = dot(left, att_all[...].reshape(rows_all, 2 * width), TN)
            for n in range(2):
                for c in range(2):
                    base = (2 * n + c) * out_rows
                    for x in range(2):
                        rows = piece[base:base + out_rows, x * width:(x + 1) * width]
                        part[c, n, x, p, m] = rows

    def w_pair(p):
        return remote(wp_send.at[p], wp_recv.at[p], w_ss.at[p], w_rs.at[p], (mate, f))

    ring_x = ((xh, ol), (1 - xh, xl), (1 - xh, ol))

    def w_cross(p, n):
        xh_there, xl_there = ring_x[n]
        to = ((2 * z + xh_there) * 2 + core, 2 * yy + xl_there)
        at = PARTS + 3 * p + n
        return remote(wx_send.at[p, n], wx_recv.at[p, n], w_ss.at[at], w_rs.at[at], to)

    def w_level(p, m):
        to = (2 * (PARTS * m + p) + xh) * 2 + core
        return remote(wz_send.at[p, m], wz_recv.at[z], w_ss.at[4 * PARTS], w_rs.at[4 * PARTS], (to, f))

    def w_levels():
        every = wz_recv.at[pl.ds(0, levels - 1)]
        return remote(every, every, w_ss.at[4 * PARTS], w_rs.at[4 * PARTS], (mate, f))

    def w_pair_start(p):
        @pl.loop(0, levels_of_part)
        def _(m):
            for n in range(2):
                for x in range(2):
                    wp_send[p, n, x, m] = part[1 - core, n, x, p, m].astype(BF16)

        w_pair(p).start()

    def w_cross_start(p):
        w_pair(p).wait_recv()
        for n in (1, 0, 2):
            xh_there, xl_there = ring_x[n]

            @pl.loop(0, levels_of_part)
            def _(m):
                total = part[core, xh_there, xl_there, p, m]
                total = total + wp_recv[p, xh_there, xl_there, m].astype(F32)
                wx_send[p, n, m] = total.astype(BF16)

            w_cross(p, n).start()

    def w_level_start(p):
        for n in range(3):
            w_cross(p, n).wait_recv()

        @pl.loop(0, levels_of_part)
        def _(m):
            total = part[core, xh, xl, p, m] + wp_recv[p, xh, xl, m].astype(F32)
            for n in range(3):
                total = total + wx_recv[p, n, m].astype(F32)
            wz_send[p, m] = total.astype(BF16)

        @pl.when(z % PARTS == p)
        def _():
            wz_recv[z] = wz_send[p, z // PARTS]

        @pl.loop(0, levels_of_part)
        def _(j):
            m = (z // PARTS + j) % levels_of_part

            @pl.when(PARTS * m + p != z)
            def _():
                w_level(p, m).start()

    at_every().wait_recv()
    w_part(0)
    w_pair_start(0)
    for p in range(1, PARTS):
        w_part(p)
        w_pair_start(p)
        w_cross_start(p - 1)
    qg[1].run()
    qg[2].run()
    w_cross_start(PARTS - 1)
    qg[3].run()
    local_pair(2)
    local_pair(3)
    qg[0].finish()
    w_level_start(0)
    w_level_start(1)

    def final_pair(n):
        for column in pairs[n]:
            for u in range(2):
                h = 2 * column + u
                after = state[1, h]
                grad = dot(v_of(h), after, NT) + acc_k[:, head_cols(h)]
                kg_ref[:, head_cols(h)] = (factor * grad).astype(BF16)
                grad = dot(k_of(h), after) + acc_v[:, head_cols(h)]
                vg_ref[:, head_cols(h)] = (factor * grad).astype(BF16)

    for n in range(1, 3):
        qg[n].finish()
    for n in range(3):
        qg[n].wait()
        final_pair(n)
    w_level_start(2)
    qg[3].finish()
    w_level_start(3)
    qg[3].wait()
    final_pair(3)
    for copy in (*own, *past_up, *past_down):
        copy.wait_send()

    for n, row in enumerate((up, down, far)):
        g_copy(n, row).wait_send()
    w_side.wait_send()
    w_share.wait_send()
    at_every().wait_send()
    kv.drain()
    for scan in qg:
        scan.drain()
    for p in range(PARTS):
        w_pair(p).wait_send()
        for n in range(3):
            w_cross(p, n).wait_send()
    w_levels().wait_recv()
    total = wz_recv[0].astype(F32)
    for j in range(1, levels):
        total = total + wz_recv[j].astype(F32)
    wg_ref[...] = total * grad_factor
    w_levels().wait_send()


def store(*refs):
    sems = refs[-1]
    copies = [pltpu.make_async_copy(refs[i], refs[4 + i], sems.at[i]) for i in range(4)]
    for copy in copies:
        copy.start()
    for copy in copies:
        copy.wait()


def body(queries, key_vectors, value_vectors, out_grad, out_weight):
    seq_devices = lax.axis_size("seq")
    group = lax.axis_size("fsdp")
    chips = seq_devices // 2
    _, tokens, width_all = queries.shape
    depth, width = out_weight.shape
    factor = 1.0 / math.sqrt(HEAD_DIM * tokens * seq_devices)
    grad_factor = 1.0 / math.sqrt(group * tokens * seq_devices)
    half = HEADS // 2
    out_rows = depth // seq_devices
    flat = (tokens, width_all)
    vmem = pl.BlockSpec(memory_space=pltpu.VMEM)
    levels = chips // 2
    ring = group // 2
    pieces = (levels // PARTS, out_rows, width)
    blocks = pltpu.VMEM((group, tokens, width), BF16)
    square = (HEAD_DIM, HEAD_DIM)
    chunk = (4, 2)
    dma = pltpu.SemaphoreType.DMA
    shapes = (
        jax.ShapeDtypeStruct(flat, BF16),
        jax.ShapeDtypeStruct(flat, BF16),
        jax.ShapeDtypeStruct(flat, BF16),
        jax.ShapeDtypeStruct((out_rows, width), F32),
    )
    args = [x.reshape(flat) for x in (queries, key_vectors, value_vectors, out_grad)]
    args = [pltpu.with_memory_space_constraint(x, pltpu.HBM) for x in (*args, out_weight)]
    results = pl.pallas_call(
        functools.partial(kernel, chips, group // 2, factor, grad_factor),
        out_shape=shapes,
        in_specs=[pl.BlockSpec(memory_space=pltpu.HBM)] * 5,
        out_specs=(vmem,) * 4,
        scratch_shapes=[
            pltpu.VMEM(flat, BF16),
            pltpu.VMEM(flat, BF16),
            pltpu.VMEM(flat, BF16),
            pltpu.VMEM((2, depth, width), BF16),
            pltpu.VMEM((ring, tokens, depth), BF16),
            blocks,
            pltpu.VMEM((3, 2, tokens, width), BF16),
            pltpu.VMEM((ring, tokens, 2 * width), BF16),
            pltpu.VMEM((ring, tokens, 2 * width), BF16),
            pltpu.VMEM((half,) + square, F32),
            pltpu.VMEM((half,) + square, F32),
            pltpu.VMEM((half,) + square, F32),
            pltpu.VMEM((4, chips, half * HEAD_DIM // chips, HEAD_DIM), BF16),
            pltpu.VMEM((half,) + square, BF16),
            pltpu.VMEM(chunk + square, F32),
            pltpu.VMEM(chunk + square, F32),
            pltpu.VMEM(chunk + square, F32),
            pltpu.VMEM((4, 4, chips, 2 * HEAD_DIM // chips, HEAD_DIM), BF16),
            pltpu.VMEM(chunk + square, BF16),
            pltpu.VMEM((2, HEADS) + square, BF16),
            pltpu.VMEM(flat, F32),
            pltpu.VMEM(flat, F32),
            pltpu.VMEM(flat, F32),
            pltpu.VMEM((2, 2, 2, PARTS, levels // PARTS, out_rows, width), F32),
            pltpu.VMEM((PARTS, 2, 2) + pieces, BF16),
            pltpu.VMEM((PARTS, 2, 2) + pieces, BF16),
            pltpu.VMEM((PARTS, 3) + pieces, BF16),
            pltpu.VMEM((PARTS, 3) + pieces, BF16),
            pltpu.VMEM((PARTS,) + pieces, BF16),
            pltpu.VMEM((levels, out_rows, width), BF16),
            dma((5,)),
            dma((3, 4)),
            dma((ring, 4)),
            dma((3,)),
            dma((ring,)),
            dma((1,)),
            dma((1,)),
            dma((10,)),
            dma((10,)),
            dma((10,)),
            dma((10,)),
            dma((4 * PARTS + 3,)),
            dma((4 * PARTS + 3,)),
        ],
        compiler_params=pltpu.CompilerParams(
            collective_id=0, has_side_effects=True, vmem_limit_bytes=44 * 1024 * 1024
        ),
    )(*args)
    results = pl.pallas_call(
        store,
        out_shape=shapes,
        in_specs=[vmem] * 4,
        out_specs=(pl.BlockSpec(memory_space=pltpu.HBM),) * 4,
        scratch_shapes=[dma((4,))],
        compiler_params=pltpu.CompilerParams(vmem_limit_bytes=16 * 1024 * 1024),
    )(*results)
    whole = (1,) + flat
    return (
        results[0].reshape(whole),
        results[1].reshape(whole),
        results[2].reshape(whole),
        results[3],
    )


def solution(mesh):
    in_specs = (
        P("fsdp", "seq", None),
        P("fsdp", "seq", None),
        P("fsdp", "seq", None),
        P("fsdp", "seq", None),
        P(None, "fsdp"),
    )
    out_specs = (
        P("fsdp", "seq", None),
        P("fsdp", "seq", None),
        P("fsdp", "seq", None),
        P("seq", "fsdp"),
    )
    return jax.shard_map(body, mesh=mesh, in_specs=in_specs, out_specs=out_specs, check_vma=False)
```

```python
import functools
import math

import jax
import jax.numpy as jnp
from jax import lax
from jax.experimental import pallas as pl
from jax.experimental.pallas import tpu as pltpu
from jax.sharding import PartitionSpec as P

HEADS = 16
HEAD_DIM = 128
BLOCK = 128
PARTS = 4
MESH = pl.DeviceIdType.MESH
F32 = jnp.float32
BF16 = jnp.bfloat16
NT = (((1,), (1,)), ((), ()))
TN = (((0,), (0,)), ((), ()))


def dot(a, b, dims=(((1,), (0,)), ((), ()))):
    return lax.dot_general(a, b, dims, preferred_element_type=F32)


def head_cols(h):
    return pl.ds(pl.multiple_of(h * HEAD_DIM, HEAD_DIM), HEAD_DIM)


def kernel(
    chips,
    ring,
    factor,
    grad_factor,
    q_in,
    k_in,
    v_in,
    og_in,
    w_in,
    qg_ref,
    kg_ref,
    vg_ref,
    wg_ref,
    q_ref,
    k_ref,
    v_ref,
    w_all,
    og_all,
    gbuf,
    gsend,
    att_all,
    att_send,
    contrib0,
    xc_send0,
    xc_recv0,
    slices0,
    p_out0,
    contrib1,
    xc_send1,
    xc_recv1,
    slices1,
    p_out1,
    state,
    acc_a,
    acc_k,
    acc_v,
    part,
    wp_send,
    wp_recv,
    wx_send,
    wx_recv,
    wz_send,
    wz_recv,
    in_sem,
    ag_ss,
    ag_rs,
    g_ss,
    g_rs,
    at_ss,
    at_rs,
    x_ss,
    x_rs,
    a_ss,
    a_rs,
    w_ss,
    w_rs,
):
    s = lax.axis_index("seq")
    f = lax.axis_index("fsdp")
    group = 2 * ring
    half = HEADS // 2
    chip, core = s // 2, s % 2
    levels = chips // 2
    z, xh = chip // 2, chip % 2
    across = (2 * z + 1 - xh) * 2 + core
    mate = s + 1 - 2 * core
    yy, xl = f // 2, f % 2
    xp = f + 1 - 2 * xl
    up = ((yy + 1) % ring) * 2
    down = ((yy + ring - 1) % ring) * 2
    far = ((yy + 2) % ring) * 2
    ol = 1 - xl

    def remote(src, dst, ssem, rsem, dev):
        return pltpu.make_async_remote_copy(
            src_ref=src,
            dst_ref=dst,
            send_sem=ssem,
            recv_sem=rsem,
            device_id=dev,
            device_id_type=MESH,
        )

    load_k = pltpu.make_async_copy(k_in, k_ref, in_sem.at[0])
    load_v = pltpu.make_async_copy(v_in, v_ref, in_sem.at[1])
    load_og = pltpu.make_async_copy(og_in, og_all.at[yy], in_sem.at[2])
    load_w = pltpu.make_async_copy(w_in, w_all.at[xl], in_sem.at[3])
    load_q = pltpu.make_async_copy(q_in, q_ref, in_sem.at[4])
    for load in (load_k, load_v, load_og, load_w, load_q):
        load.start()
    barrier = pltpu.get_barrier_semaphore()

    @pl.loop(1, ring)
    def _(j):
        row = (2 * yy + 2 * j) % group
        pl.semaphore_signal(barrier, inc=1, device_id=(s, row + xl), device_id_type=MESH)

    @pl.loop(1, chips)
    def _(j):
        other = ((chip + j) % chips) * 2 + core
        pl.semaphore_signal(barrier, inc=1, device_id=(other, f), device_id_type=MESH)

    pl.semaphore_signal(barrier, inc=1, device_id=(mate, f), device_id_type=MESH)
    pl.semaphore_signal(barrier, inc=1, device_id=(across, xp), device_id_type=MESH)
    pl.semaphore_signal(barrier, inc=1, device_id=(s, xp), device_id_type=MESH)
    pl.semaphore_wait(barrier, ring - 1 + chips - 1 + 3)

    def quarter_view(ref, part_at):
        return ref.at[pl.ds(part_at * (BLOCK // 4), BLOCK // 4)]

    def ag_own(n, part_at, dev):
        return remote(
            quarter_view(og_in, part_at), quarter_view(og_all.at[yy], part_at),
            ag_ss.at[n, part_at], ag_rs.at[yy, part_at], (s, dev),
        )

    def ag_pass(n, slot, part_at, dev):
        view = quarter_view(og_all.at[slot], part_at)
        return remote(view, view, ag_ss.at[n, part_at], ag_rs.at[slot, part_at], (s, dev))

    def ag_wait(slot, *parts_at):
        for part_at in parts_at:
            ag_pass(0, slot, part_at, xp).wait_recv()

    own = [ag_own(0, p, up + xl) for p in range(4)] + [ag_own(1, p, down + xl) for p in (3, 2, 1, 0)]
    past_up = [ag_pass(2, down // 2, p, up + xl) for p in (0, 1)]
    past_down = [ag_pass(2, up // 2, p, down + xl) for p in (3, 2)]

    w_part = w_in.shape[0] // 2
    w_rows_here = pl.ds(core * w_part, w_part)
    w_rows_mate = pl.ds((1 - core) * w_part, w_part)
    w_side = remote(
        w_in.at[w_rows_here], w_all.at[xl, w_rows_here], w_ss.at[4 * PARTS + 1], w_rs.at[4 * PARTS + 1], (across, xp)
    )
    w_got = w_all.at[1 - xl, w_rows_here]
    w_share = remote(w_got, w_got, w_ss.at[4 * PARTS + 2], w_rs.at[4 * PARTS + 2], (mate, f))

    w_side.start()
    for p in range(4):
        own[p].start()
        own[4 + p].start()

    def q_of(h):
        return q_ref[:, head_cols(h)]

    def k_of(h):
        return k_ref[:, head_cols(h)]

    def v_of(h):
        return v_ref[:, head_cols(h)]

    def g_of(h):
        return gbuf[h // 2, :, pl.ds(pl.multiple_of((h % 2) * HEAD_DIM, HEAD_DIM), HEAD_DIM)]

    def a2a_copy(src, dst, n, there):
        return remote(src, dst, a_ss.at[n], a_rs.at[n], (there * 2 + core, f))

    def a2a_start(src, dst, n):
        @pl.loop(1, chips)
        def _(j):
            there = (chip + j) % chips
            a2a_copy(src.at[there], dst.at[chip], n, there).start()

    def a2a_all(src, dst, n):
        every = pl.ds(0, chips - 1)
        return remote(src.at[every], dst.at[every], a_ss.at[n], a_rs.at[n], (mate, f))

    def a2a_wait(src, dst, n):
        a2a_all(src, dst, n).wait_recv()

    def a2a_drain(src, dst, n):
        a2a_all(src, dst, n).wait_send()

    class Scan:
        def __init__(self, at, b, reverse, mine, other, left, right, bufs):
            self.at, self.b, self.reverse = at, b, reverse
            self.mine, self.other, self.left, self.right = mine, other, left, right
            self.contrib, self.xc_send, self.xc_recv, slices, self.p_out = bufs
            self.a_send, self.a_recv, self.r_send, self.r_recv = [slices.at[i] for i in range(4)]
            self.heads = self.contrib.shape[0]
            self.rows = self.heads * HEAD_DIM // chips

        def pair(self):
            return remote(
                self.xc_send, self.xc_recv, x_ss.at[2 * self.at], x_rs.at[2 * self.at], (mate, f)
            )

        def place(self, j):
            row = pl.multiple_of((j * self.rows) % HEAD_DIM, self.rows)
            return j * self.rows // HEAD_DIM, pl.ds(row, self.rows)

        def start(self):
            @pl.loop(0, self.heads // 2)
            def _(i):
                for u in range(2):
                    h = self.other + 2 * i + u
                    self.xc_send[2 * i + u] = dot(self.left(h), self.right(h), TN)

            self.pair().start()

            @pl.loop(0, self.heads // 2)
            def _(i):
                for u in range(2):
                    h = self.mine + 2 * i + u
                    self.contrib[2 * i + u] = dot(self.left(h), self.right(h), TN)

        def spread(self):
            self.pair().wait_recv()

            @pl.loop(0, chips)
            def _(j):
                head, rows = self.place(j)
                self.a_send[j] = (self.contrib[head, rows] + self.xc_recv[head, rows]).astype(BF16)

            self.a_recv[chip] = self.a_send[chip]
            a2a_start(self.a_send, self.a_recv, 2 * self.at)

        def run(self):
            a2a_wait(self.a_send, self.a_recv, 2 * self.at)
            total = jnp.zeros((self.rows, HEAD_DIM), F32)
            for j in range(chips):
                at = chips - 1 - j if self.reverse else j
                self.r_send[at] = total.astype(BF16)
                total = total + self.a_recv[at].astype(F32)
            self.r_recv[chip] = self.r_send[chip]
            a2a_start(self.r_send, self.r_recv, 2 * self.at + 1)

        def back(self):
            heads = pl.ds(self.mine, self.heads)
            return remote(
                self.p_out, state.at[self.b, heads],
                x_ss.at[2 * self.at + 1], x_rs.at[2 * self.at + 1], (mate, f),
            )

        def finish(self):
            a2a_wait(self.r_send, self.r_recv, 2 * self.at + 1)
            first = core == (1 if self.reverse else 0)

            @pl.loop(0, chips)
            def _(j):
                head, rows = self.place(j)
                carried = self.r_recv[j].astype(F32)
                mine, theirs = self.contrib[head, rows], self.xc_recv[head, rows]
                self.p_out[head, rows] = (carried + jnp.where(first, mine, 0.0)).astype(BF16)
                state[self.b, self.mine + head, rows] = (
                    carried + jnp.where(first, 0.0, theirs)
                ).astype(BF16)

            self.back().start()

        def wait(self):
            heads = pl.ds(self.other, self.heads)
            remote(
                self.p_out, state.at[self.b, heads],
                x_ss.at[2 * self.at + 1], x_rs.at[2 * self.at + 1], (mate, f),
            ).wait_recv()

        def drain(self):
            self.pair().wait_send()
            self.back().wait_send()
            a2a_drain(self.a_send, self.a_recv, 2 * self.at)
            a2a_drain(self.r_send, self.r_recv, 2 * self.at + 1)

    kv = Scan(
        0, 0, False, core * half, (1 - core) * half, k_of, v_of,
        (contrib0, xc_send0, xc_recv0, slices0, p_out0),
    )
    pairs = tuple((row, row + 1) for row in (2 * yy, up, down, far))
    qg = []
    for n, (first, second) in enumerate(pairs):
        mine = 2 * (first + core * (second - first))
        other = 2 * (second + core * (first - second))
        bufs = tuple(ref.at[n] for ref in (contrib1, xc_send1, xc_recv1, slices1, p_out1))
        qg.append(Scan(1 + n, 1, True, mine, other, q_of, g_of, bufs))

    load_k.wait()
    load_v.wait()
    kv.start()
    kv.spread()

    def g_copy(n, row):
        to = gbuf.at[pl.ds(2 * yy, 2)]
        return remote(gsend.at[n], to, g_ss.at[n], g_rs.at[yy], (s, row + xl))

    def g_make(n, row):
        for c in range(2):
            gsend[n, c] = dot(og_all[row // 2], w_all[c]).astype(BF16)

    def g_wait(row):
        at = gbuf.at[pl.ds(row, 2)]
        remote(gsend.at[0], at, g_ss.at[0], g_rs.at[row // 2], (s, row + xl)).wait_recv()

    row_index = lax.broadcasted_iota(jnp.int32, (BLOCK, BLOCK), 0)
    col_index = lax.broadcasted_iota(jnp.int32, (BLOCK, BLOCK), 1)
    lower = row_index >= col_index
    upper = row_index <= col_index
    load_q.wait()

    @pl.loop(0, HEADS // 2)
    def _(i):
        for u in range(2):
            h = 2 * i + u
            scores = jnp.where(lower, dot(q_of(h), k_of(h), NT), 0.0).astype(BF16)
            acc_a[:, head_cols(h)] = dot(scores, v_of(h))

    for n in range(2):
        ag_wait(down // 2, n)
        past_up[n].start()
        ag_wait(up // 2, 3 - n)
        past_down[n].start()
    kv.run()
    remote(
        w_in.at[w_rows_here], w_got, w_ss.at[4 * PARTS + 1], w_rs.at[4 * PARTS + 1], (across, xp)
    ).wait_recv()
    w_share.start()
    load_og.wait()
    load_w.wait()
    ag_wait(down // 2, 2, 3)
    ag_wait(up // 2, 1, 0)
    w_theirs = w_all.at[1 - xl, w_rows_mate]
    remote(w_theirs, w_theirs, w_ss.at[4 * PARTS + 2], w_rs.at[4 * PARTS + 2], (mate, f)).wait_recv()
    for c in range(2):
        gbuf[2 * yy + c] = dot(og_all[yy], w_all[c]).astype(BF16)
    g_make(0, up)
    g_copy(0, up).start()
    g_make(1, down)
    g_copy(1, down).start()

    def local_grads(h):
        q, k, v, g = q_of(h), k_of(h), v_of(h), g_of(h)
        mixing = jnp.where(lower, dot(g, v, NT), 0.0).astype(BF16)
        grad = dot(mixing, k) + dot(g, state[0, h], NT)
        qg_ref[:, head_cols(h)] = (factor * grad).astype(BF16)
        mixing_t = jnp.where(upper, dot(v, g, NT), 0.0).astype(BF16)
        acc_k[:, head_cols(h)] = dot(mixing_t, q)
        scores_t = jnp.where(upper, dot(k, q, NT), 0.0).astype(BF16)
        acc_v[:, head_cols(h)] = dot(scores_t, g)

    def local_pair(n):
        for column in pairs[n]:
            for u in range(2):
                local_grads(2 * column + u)

    def at_copy(row):
        return remote(
            att_send.at[row // 2], att_all.at[yy], at_ss.at[0], at_rs.at[0], (s, row + xl)
        )

    def at_every():
        some = pl.ds(0, ring - 1)
        return remote(att_send.at[some], att_all.at[some], at_ss.at[0], at_rs.at[0], (mate, f))

    qg[0].start()
    qg[0].spread()
    ag_wait(far // 2, 0, 3, 1, 2)
    g_make(2, far)
    g_copy(2, far).start()
    kv.finish()
    kv.wait()
    @pl.loop(0, ring)
    def _(i):
        for u in range(HEADS // ring):
            h = i * (HEADS // ring) + u
            attended = dot(q_of(h), state[0, h]) + acc_a[:, head_cols(h)]
            att_send[i, :, u * HEAD_DIM:(u + 1) * HEAD_DIM] = (factor * attended).astype(BF16)

    att_all[yy] = att_send[yy]
    for row in (up, down, far):
        at_copy(row).start()
    local_pair(0)
    g_wait(up)
    qg[1].start()
    qg[1].spread()
    g_wait(down)
    qg[2].start()
    qg[2].spread()
    local_pair(1)
    qg[0].run()
    g_wait(far)
    qg[3].start()
    qg[3].spread()

    depth, width = w_in.shape
    out_rows = wg_ref.shape[0]
    step = 256
    rows_all = ring * BLOCK
    levels_of_part = levels // PARTS

    def w_part(p):
        @pl.loop(0, levels_of_part)
        def _(m):
            cols = pl.ds(pl.multiple_of((PARTS * m + p) * step, step), step)
            left = og_all[:, :, cols].reshape(rows_all, step)
            piece = dot(left, att_all[...].reshape(rows_all, 2 * width), TN)
            for n in range(2):
                for c in range(2):
                    base = (2 * n + c) * out_rows
                    for x in range(2):
                        rows = piece[base:base + out_rows, x * width:(x + 1) * width]
                        part[c, n, x, p, m] = rows

    def w_pair(p):
        return remote(wp_send.at[p], wp_recv.at[p], w_ss.at[p], w_rs.at[p], (mate, f))

    ring_x = ((xh, ol), (1 - xh, xl), (1 - xh, ol))

    def w_cross(p, n):
        xh_there, xl_there = ring_x[n]
        to = ((2 * z + xh_there) * 2 + core, 2 * yy + xl_there)
        at = PARTS + 3 * p + n
        return remote(wx_send.at[p, n], wx_recv.at[p, n], w_ss.at[at], w_rs.at[at], to)

    def w_level(p, m):
        to = (2 * (PARTS * m + p) + xh) * 2 + core
        return remote(wz_send.at[p, m], wz_recv.at[z], w_ss.at[4 * PARTS], w_rs.at[4 * PARTS], (to, f))

    def w_levels():
        every = wz_recv.at[pl.ds(0, levels - 1)]
        return remote(every, every, w_ss.at[4 * PARTS], w_rs.at[4 * PARTS], (mate, f))

    def w_pair_start(p):
        @pl.loop(0, levels_of_part)
        def _(m):
            for n in range(2):
                for x in range(2):
                    wp_send[p, n, x, m] = part[1 - core, n, x, p, m].astype(BF16)

        w_pair(p).start()

    def w_cross_start(p):
        w_pair(p).wait_recv()
        for n in (1, 0, 2):
            xh_there, xl_there = ring_x[n]

            @pl.loop(0, levels_of_part)
            def _(m):
                total = part[core, xh_there, xl_there, p, m]
                total = total + wp_recv[p, xh_there, xl_there, m].astype(F32)
                wx_send[p, n, m] = total.astype(BF16)

            w_cross(p, n).start()

    def w_level_start(p):
        for n in range(3):
            w_cross(p, n).wait_recv()

        @pl.loop(0, levels_of_part)
        def _(m):
            total = part[core, xh, xl, p, m] + wp_recv[p, xh, xl, m].astype(F32)
            for n in range(3):
                total = total + wx_recv[p, n, m].astype(F32)
            wz_send[p, m] = total.astype(BF16)

        @pl.when(z % PARTS == p)
        def _():
            wz_recv[z] = wz_send[p, z // PARTS]

        @pl.loop(0, levels_of_part)
        def _(j):
            m = (z // PARTS + j) % levels_of_part

            @pl.when(PARTS * m + p != z)
            def _():
                w_level(p, m).start()

    at_every().wait_recv()
    w_part(0)
    w_pair_start(0)
    for p in range(1, PARTS):
        w_part(p)
        w_pair_start(p)
        w_cross_start(p - 1)
    qg[1].run()
    qg[2].run()
    w_cross_start(PARTS - 1)
    qg[3].run()
    local_pair(2)
    local_pair(3)
    qg[0].finish()
    w_level_start(0)
    w_level_start(1)
    w_level_start(2)

    def final_pair(n):
        for column in pairs[n]:
            for u in range(2):
                h = 2 * column + u
                after = state[1, h]
                grad = dot(v_of(h), after, NT) + acc_k[:, head_cols(h)]
                kg_ref[:, head_cols(h)] = (factor * grad).astype(BF16)
                grad = dot(k_of(h), after) + acc_v[:, head_cols(h)]
                vg_ref[:, head_cols(h)] = (factor * grad).astype(BF16)

    for n in range(1, 3):
        qg[n].finish()
    w_level_start(3)
    for n in range(3):
        qg[n].wait()
        final_pair(n)
    qg[3].finish()
    qg[3].wait()
    final_pair(3)
    for copy in (*own, *past_up, *past_down):
        copy.wait_send()

    for n, row in enumerate((up, down, far)):
        g_copy(n, row).wait_send()
    w_side.wait_send()
    w_share.wait_send()
    at_every().wait_send()
    kv.drain()
    for scan in qg:
        scan.drain()
    for p in range(PARTS):
        w_pair(p).wait_send()
        for n in range(3):
            w_cross(p, n).wait_send()
    w_levels().wait_recv()
    total = wz_recv[0].astype(F32)
    for j in range(1, levels):
        total = total + wz_recv[j].astype(F32)
    wg_ref[...] = total * grad_factor
    w_levels().wait_send()


def store(*refs):
    sems = refs[-1]
    copies = [pltpu.make_async_copy(refs[i], refs[4 + i], sems.at[i]) for i in range(4)]
    for copy in copies:
        copy.start()
    for copy in copies:
        copy.wait()


def body(queries, key_vectors, value_vectors, out_grad, out_weight):
    seq_devices = lax.axis_size("seq")
    group = lax.axis_size("fsdp")
    chips = seq_devices // 2
    _, tokens, width_all = queries.shape
    depth, width = out_weight.shape
    factor = 1.0 / math.sqrt(HEAD_DIM * tokens * seq_devices)
    grad_factor = 1.0 / math.sqrt(group * tokens * seq_devices)
    half = HEADS // 2
    out_rows = depth // seq_devices
    flat = (tokens, width_all)
    vmem = pl.BlockSpec(memory_space=pltpu.VMEM)
    levels = chips // 2
    ring = group // 2
    pieces = (levels // PARTS, out_rows, width)
    blocks = pltpu.VMEM((group, tokens, width), BF16)
    square = (HEAD_DIM, HEAD_DIM)
    chunk = (4, 2)
    dma = pltpu.SemaphoreType.DMA
    shapes = (
        jax.ShapeDtypeStruct(flat, BF16),
        jax.ShapeDtypeStruct(flat, BF16),
        jax.ShapeDtypeStruct(flat, BF16),
        jax.ShapeDtypeStruct((out_rows, width), F32),
    )
    args = [x.reshape(flat) for x in (queries, key_vectors, value_vectors, out_grad)]
    args = [pltpu.with_memory_space_constraint(x, pltpu.HBM) for x in (*args, out_weight)]
    results = pl.pallas_call(
        functools.partial(kernel, chips, group // 2, factor, grad_factor),
        out_shape=shapes,
        in_specs=[pl.BlockSpec(memory_space=pltpu.HBM)] * 5,
        out_specs=(vmem,) * 4,
        scratch_shapes=[
            pltpu.VMEM(flat, BF16),
            pltpu.VMEM(flat, BF16),
            pltpu.VMEM(flat, BF16),
            pltpu.VMEM((2, depth, width), BF16),
            pltpu.VMEM((ring, tokens, depth), BF16),
            blocks,
            pltpu.VMEM((3, 2, tokens, width), BF16),
            pltpu.VMEM((ring, tokens, 2 * width), BF16),
            pltpu.VMEM((ring, tokens, 2 * width), BF16),
            pltpu.VMEM((half,) + square, F32),
            pltpu.VMEM((half,) + square, F32),
            pltpu.VMEM((half,) + square, F32),
            pltpu.VMEM((4, chips, half * HEAD_DIM // chips, HEAD_DIM), BF16),
            pltpu.VMEM((half,) + square, BF16),
            pltpu.VMEM(chunk + square, F32),
            pltpu.VMEM(chunk + square, F32),
            pltpu.VMEM(chunk + square, F32),
            pltpu.VMEM((4, 4, chips, 2 * HEAD_DIM // chips, HEAD_DIM), BF16),
            pltpu.VMEM(chunk + square, BF16),
            pltpu.VMEM((2, HEADS) + square, BF16),
            pltpu.VMEM(flat, F32),
            pltpu.VMEM(flat, F32),
            pltpu.VMEM(flat, F32),
            pltpu.VMEM((2, 2, 2, PARTS, levels // PARTS, out_rows, width), F32),
            pltpu.VMEM((PARTS, 2, 2) + pieces, BF16),
            pltpu.VMEM((PARTS, 2, 2) + pieces, BF16),
            pltpu.VMEM((PARTS, 3) + pieces, BF16),
            pltpu.VMEM((PARTS, 3) + pieces, BF16),
            pltpu.VMEM((PARTS,) + pieces, BF16),
            pltpu.VMEM((levels, out_rows, width), BF16),
            dma((5,)),
            dma((3, 4)),
            dma((ring, 4)),
            dma((3,)),
            dma((ring,)),
            dma((1,)),
            dma((1,)),
            dma((10,)),
            dma((10,)),
            dma((10,)),
            dma((10,)),
            dma((4 * PARTS + 3,)),
            dma((4 * PARTS + 3,)),
        ],
        compiler_params=pltpu.CompilerParams(
            collective_id=0, has_side_effects=True, vmem_limit_bytes=44 * 1024 * 1024
        ),
    )(*args)
    results = pl.pallas_call(
        store,
        out_shape=shapes,
        in_specs=[vmem] * 4,
        out_specs=(pl.BlockSpec(memory_space=pltpu.HBM),) * 4,
        scratch_shapes=[dma((4,))],
        compiler_params=pltpu.CompilerParams(vmem_limit_bytes=16 * 1024 * 1024),
    )(*results)
    whole = (1,) + flat
    return (
        results[0].reshape(whole),
        results[1].reshape(whole),
        results[2].reshape(whole),
        results[3],
    )


def solution(mesh):
    in_specs = (
        P("fsdp", "seq", None),
        P("fsdp", "seq", None),
        P("fsdp", "seq", None),
        P("fsdp", "seq", None),
        P(None, "fsdp"),
    )
    out_specs = (
        P("fsdp", "seq", None),
        P("fsdp", "seq", None),
        P("fsdp", "seq", None),
        P("seq", "fsdp"),
    )
    return jax.shard_map(body, mesh=mesh, in_specs=in_specs, out_specs=out_specs, check_vma=False)
```

```python
import functools
import math

import jax
import jax.numpy as jnp
from jax import lax
from jax.experimental import pallas as pl
from jax.experimental.pallas import tpu as pltpu
from jax.sharding import PartitionSpec as P

HEADS = 16
HEAD_DIM = 128
BLOCK = 128
PARTS = 4
MESH = pl.DeviceIdType.MESH
F32 = jnp.float32
BF16 = jnp.bfloat16
NT = (((1,), (1,)), ((), ()))
TN = (((0,), (0,)), ((), ()))


def dot(a, b, dims=(((1,), (0,)), ((), ()))):
    return lax.dot_general(a, b, dims, preferred_element_type=F32)


def head_cols(h):
    return pl.ds(pl.multiple_of(h * HEAD_DIM, HEAD_DIM), HEAD_DIM)


def kernel(
    chips,
    ring,
    factor,
    grad_factor,
    q_in,
    k_in,
    v_in,
    og_in,
    w_in,
    qg_ref,
    kg_ref,
    vg_ref,
    wg_ref,
    q_ref,
    k_ref,
    v_ref,
    w_all,
    og_all,
    gbuf,
    gsend,
    att_all,
    att_send,
    contrib0,
    xc_send0,
    xc_recv0,
    slices0,
    p_out0,
    contrib1,
    xc_send1,
    xc_recv1,
    slices1,
    p_out1,
    state,
    acc_a,
    acc_k,
    acc_v,
    part,
    wp_send,
    wp_recv,
    wx_send,
    wx_recv,
    wz_send,
    wz_recv,
    in_sem,
    ag_ss,
    ag_rs,
    g_ss,
    g_rs,
    at_ss,
    at_rs,
    x_ss,
    x_rs,
    a_ss,
    a_rs,
    w_ss,
    w_rs,
):
    s = lax.axis_index("seq")
    f = lax.axis_index("fsdp")
    group = 2 * ring
    half = HEADS // 2
    chip, core = s // 2, s % 2
    levels = chips // 2
    z, xh = chip // 2, chip % 2
    across = (2 * z + 1 - xh) * 2 + core
    mate = s + 1 - 2 * core
    yy, xl = f // 2, f % 2
    xp = f + 1 - 2 * xl
    up = ((yy + 1) % ring) * 2
    down = ((yy + ring - 1) % ring) * 2
    far = ((yy + 2) % ring) * 2
    ol = 1 - xl

    def remote(src, dst, ssem, rsem, dev):
        return pltpu.make_async_remote_copy(
            src_ref=src,
            dst_ref=dst,
            send_sem=ssem,
            recv_sem=rsem,
            device_id=dev,
            device_id_type=MESH,
        )

    load_k = pltpu.make_async_copy(k_in, k_ref, in_sem.at[0])
    load_v = pltpu.make_async_copy(v_in, v_ref, in_sem.at[1])
    load_og = pltpu.make_async_copy(og_in, og_all.at[yy], in_sem.at[2])
    load_w = pltpu.make_async_copy(w_in, w_all.at[xl], in_sem.at[3])
    load_q = pltpu.make_async_copy(q_in, q_ref, in_sem.at[4])
    for load in (load_k, load_v, load_og, load_w, load_q):
        load.start()
    barrier = pltpu.get_barrier_semaphore()

    @pl.loop(1, ring)
    def _(j):
        row = (2 * yy + 2 * j) % group
        pl.semaphore_signal(barrier, inc=1, device_id=(s, row + xl), device_id_type=MESH)

    @pl.loop(1, chips)
    def _(j):
        other = ((chip + j) % chips) * 2 + core
        pl.semaphore_signal(barrier, inc=1, device_id=(other, f), device_id_type=MESH)

    pl.semaphore_signal(barrier, inc=1, device_id=(mate, f), device_id_type=MESH)
    pl.semaphore_signal(barrier, inc=1, device_id=(across, xp), device_id_type=MESH)
    pl.semaphore_signal(barrier, inc=1, device_id=(s, xp), device_id_type=MESH)
    pl.semaphore_wait(barrier, ring - 1 + chips - 1 + 3)

    def quarter_view(ref, part_at):
        return ref.at[pl.ds(part_at * (BLOCK // 4), BLOCK // 4)]

    def ag_own(n, part_at, dev):
        return remote(
            quarter_view(og_in, part_at), quarter_view(og_all.at[yy], part_at),
            ag_ss.at[n, part_at], ag_rs.at[yy, part_at], (s, dev),
        )

    def ag_pass(n, slot, part_at, dev):
        view = quarter_view(og_all.at[slot], part_at)
        return remote(view, view, ag_ss.at[n, part_at], ag_rs.at[slot, part_at], (s, dev))

    def ag_wait(slot, *parts_at):
        for part_at in parts_at:
            ag_pass(0, slot, part_at, xp).wait_recv()

    own = [ag_own(0, p, up + xl) for p in range(4)] + [ag_own(1, p, down + xl) for p in (3, 2, 1, 0)]
    past_up = [ag_pass(2, down // 2, p, up + xl) for p in (0, 1)]
    past_down = [ag_pass(2, up // 2, p, down + xl) for p in (3, 2)]

    w_part = w_in.shape[0] // 2
    w_rows_here = pl.ds(core * w_part, w_part)
    w_rows_mate = pl.ds((1 - core) * w_part, w_part)
    w_side = remote(
        w_in.at[w_rows_here], w_all.at[xl, w_rows_here], w_ss.at[4 * PARTS + 1], w_rs.at[4 * PARTS + 1], (across, xp)
    )
    w_got = w_all.at[1 - xl, w_rows_here]
    w_share = remote(w_got, w_got, w_ss.at[4 * PARTS + 2], w_rs.at[4 * PARTS + 2], (mate, f))

    w_side.start()
    for p in range(4):
        own[p].start()
        own[4 + p].start()

    def q_of(h):
        return q_ref[:, head_cols(h)]

    def k_of(h):
        return k_ref[:, head_cols(h)]

    def v_of(h):
        return v_ref[:, head_cols(h)]

    def g_of(h):
        return gbuf[h // 2, :, pl.ds(pl.multiple_of((h % 2) * HEAD_DIM, HEAD_DIM), HEAD_DIM)]

    def a2a_copy(src, dst, n, there):
        return remote(src, dst, a_ss.at[n], a_rs.at[n], (there * 2 + core, f))

    def a2a_start(src, dst, n):
        @pl.loop(1, chips)
        def _(j):
            there = (chip + j) % chips
            a2a_copy(src.at[there], dst.at[chip], n, there).start()

    def a2a_all(src, dst, n):
        every = pl.ds(0, chips - 1)
        return remote(src.at[every], dst.at[every], a_ss.at[n], a_rs.at[n], (mate, f))

    def a2a_wait(src, dst, n):
        a2a_all(src, dst, n).wait_recv()

    def a2a_drain(src, dst, n):
        a2a_all(src, dst, n).wait_send()

    class Scan:
        def __init__(self, at, b, reverse, mine, other, left, right, bufs):
            self.at, self.b, self.reverse = at, b, reverse
            self.mine, self.other, self.left, self.right = mine, other, left, right
            self.contrib, self.xc_send, self.xc_recv, slices, self.p_out = bufs
            self.a_send, self.a_recv, self.r_send, self.r_recv = [slices.at[i] for i in range(4)]
            self.heads = self.contrib.shape[0]
            self.rows = self.heads * HEAD_DIM // chips

        def pair(self):
            return remote(
                self.xc_send, self.xc_recv, x_ss.at[2 * self.at], x_rs.at[2 * self.at], (mate, f)
            )

        def place(self, j):
            row = pl.multiple_of((j * self.rows) % HEAD_DIM, self.rows)
            return j * self.rows // HEAD_DIM, pl.ds(row, self.rows)

        def start(self):
            @pl.loop(0, self.heads // 2)
            def _(i):
                for u in range(2):
                    h = self.other + 2 * i + u
                    self.xc_send[2 * i + u] = dot(self.left(h), self.right(h), TN)

            self.pair().start()

            @pl.loop(0, self.heads // 2)
            def _(i):
                for u in range(2):
                    h = self.mine + 2 * i + u
                    self.contrib[2 * i + u] = dot(self.left(h), self.right(h), TN)

        def spread(self):
            self.pair().wait_recv()

            @pl.loop(0, chips)
            def _(j):
                head, rows = self.place(j)
                self.a_send[j] = (self.contrib[head, rows] + self.xc_recv[head, rows]).astype(BF16)

            self.a_recv[chip] = self.a_send[chip]
            a2a_start(self.a_send, self.a_recv, 2 * self.at)

        def run(self):
            a2a_wait(self.a_send, self.a_recv, 2 * self.at)
            total = jnp.zeros((self.rows, HEAD_DIM), F32)
            for j in range(chips):
                at = chips - 1 - j if self.reverse else j
                self.r_send[at] = total.astype(BF16)
                total = total + self.a_recv[at].astype(F32)
            self.r_recv[chip] = self.r_send[chip]
            a2a_start(self.r_send, self.r_recv, 2 * self.at + 1)

        def back(self):
            heads = pl.ds(self.mine, self.heads)
            return remote(
                self.p_out, state.at[self.b, heads],
                x_ss.at[2 * self.at + 1], x_rs.at[2 * self.at + 1], (mate, f),
            )

        def finish(self):
            a2a_wait(self.r_send, self.r_recv, 2 * self.at + 1)
            first = core == (1 if self.reverse else 0)

            @pl.loop(0, chips)
            def _(j):
                head, rows = self.place(j)
                carried = self.r_recv[j].astype(F32)
                mine, theirs = self.contrib[head, rows], self.xc_recv[head, rows]
                self.p_out[head, rows] = (carried + jnp.where(first, mine, 0.0)).astype(BF16)
                state[self.b, self.mine + head, rows] = (
                    carried + jnp.where(first, 0.0, theirs)
                ).astype(BF16)

            self.back().start()

        def wait(self):
            heads = pl.ds(self.other, self.heads)
            remote(
                self.p_out, state.at[self.b, heads],
                x_ss.at[2 * self.at + 1], x_rs.at[2 * self.at + 1], (mate, f),
            ).wait_recv()

        def drain(self):
            self.pair().wait_send()
            self.back().wait_send()
            a2a_drain(self.a_send, self.a_recv, 2 * self.at)
            a2a_drain(self.r_send, self.r_recv, 2 * self.at + 1)

    kv = Scan(
        0, 0, False, core * half, (1 - core) * half, k_of, v_of,
        (contrib0, xc_send0, xc_recv0, slices0, p_out0),
    )
    pairs = tuple((row, row + 1) for row in (2 * yy, up, down, far))
    qg = []
    for n, (first, second) in enumerate(pairs):
        mine = 2 * (first + core * (second - first))
        other = 2 * (second + core * (first - second))
        bufs = tuple(ref.at[n] for ref in (contrib1, xc_send1, xc_recv1, slices1, p_out1))
        qg.append(Scan(1 + n, 1, True, mine, other, q_of, g_of, bufs))

    load_k.wait()
    load_v.wait()
    kv.start()
    kv.spread()

    def g_copy(n, row):
        to = gbuf.at[pl.ds(2 * yy, 2)]
        return remote(gsend.at[n], to, g_ss.at[n], g_rs.at[yy], (s, row + xl))

    def g_make(n, row):
        for c in range(2):
            gsend[n, c] = dot(og_all[row // 2], w_all[c]).astype(BF16)

    def g_wait(row):
        at = gbuf.at[pl.ds(row, 2)]
        remote(gsend.at[0], at, g_ss.at[0], g_rs.at[row // 2], (s, row + xl)).wait_recv()

    row_index = lax.broadcasted_iota(jnp.int32, (BLOCK, BLOCK), 0)
    col_index = lax.broadcasted_iota(jnp.int32, (BLOCK, BLOCK), 1)
    lower = row_index >= col_index
    upper = row_index <= col_index
    load_q.wait()

    @pl.loop(0, HEADS // 2)
    def _(i):
        for u in range(2):
            h = 2 * i + u
            scores = jnp.where(lower, dot(q_of(h), k_of(h), NT), 0.0).astype(BF16)
            acc_a[:, head_cols(h)] = dot(scores, v_of(h))

    for n in range(2):
        ag_wait(down // 2, n)
        past_up[n].start()
        ag_wait(up // 2, 3 - n)
        past_down[n].start()
    kv.run()
    remote(
        w_in.at[w_rows_here], w_got, w_ss.at[4 * PARTS + 1], w_rs.at[4 * PARTS + 1], (across, xp)
    ).wait_recv()
    w_share.start()
    load_og.wait()
    load_w.wait()
    ag_wait(down // 2, 2, 3)
    ag_wait(up // 2, 1, 0)
    w_theirs = w_all.at[1 - xl, w_rows_mate]
    remote(w_theirs, w_theirs, w_ss.at[4 * PARTS + 2], w_rs.at[4 * PARTS + 2], (mate, f)).wait_recv()
    for c in range(2):
        gbuf[2 * yy + c] = dot(og_all[yy], w_all[c]).astype(BF16)
    g_make(0, up)
    g_copy(0, up).start()
    g_make(1, down)
    g_copy(1, down).start()

    def local_grads(h):
        q, k, v, g = q_of(h), k_of(h), v_of(h), g_of(h)
        mixing = jnp.where(lower, dot(g, v, NT), 0.0).astype(BF16)
        grad = dot(mixing, k) + dot(g, state[0, h], NT)
        qg_ref[:, head_cols(h)] = (factor * grad).astype(BF16)
        mixing_t = jnp.where(upper, dot(v, g, NT), 0.0).astype(BF16)
        acc_k[:, head_cols(h)] = dot(mixing_t, q)
        scores_t = jnp.where(upper, dot(k, q, NT), 0.0).astype(BF16)
        acc_v[:, head_cols(h)] = dot(scores_t, g)

    def local_pair(n):
        for column in pairs[n]:
            for u in range(2):
                local_grads(2 * column + u)

    def at_copy(row):
        return remote(
            att_send.at[row // 2], att_all.at[yy], at_ss.at[0], at_rs.at[0], (s, row + xl)
        )

    def at_every():
        some = pl.ds(0, ring - 1)
        return remote(att_send.at[some], att_all.at[some], at_ss.at[0], at_rs.at[0], (mate, f))

    qg[0].start()
    qg[0].spread()
    ag_wait(far // 2, 0, 3, 1, 2)
    g_make(2, far)
    g_copy(2, far).start()
    kv.finish()
    kv.wait()
    @pl.loop(0, ring)
    def _(i):
        for u in range(HEADS // ring):
            h = i * (HEADS // ring) + u
            attended = dot(q_of(h), state[0, h]) + acc_a[:, head_cols(h)]
            att_send[i, :, u * HEAD_DIM:(u + 1) * HEAD_DIM] = (factor * attended).astype(BF16)

    att_all[yy] = att_send[yy]
    for row in (up, down, far):
        at_copy(row).start()
    g_wait(up)
    qg[1].start()
    qg[1].spread()
    g_wait(down)
    qg[2].start()
    qg[2].spread()
    qg[0].run()
    g_wait(far)
    qg[3].start()
    qg[3].spread()

    depth, width = w_in.shape
    out_rows = wg_ref.shape[0]
    step = 256
    rows_all = ring * BLOCK
    levels_of_part = levels // PARTS

    def w_part(p):
        @pl.loop(0, levels_of_part)
        def _(m):
            cols = pl.ds(pl.multiple_of((PARTS * m + p) * step, step), step)
            left = og_all[:, :, cols].reshape(rows_all, step)
            piece = dot(left, att_all[...].reshape(rows_all, 2 * width), TN)
            for n in range(2):
                for c in range(2):
                    base = (2 * n + c) * out_rows
                    for x in range(2):
                        rows = piece[base:base + out_rows, x * width:(x + 1) * width]
                        part[c, n, x, p, m] = rows

    def w_pair(p):
        return remote(wp_send.at[p], wp_recv.at[p], w_ss.at[p], w_rs.at[p], (mate, f))

    ring_x = ((xh, ol), (1 - xh, xl), (1 - xh, ol))

    def w_cross(p, n):
        xh_there, xl_there = ring_x[n]
        to = ((2 * z + xh_there) * 2 + core, 2 * yy + xl_there)
        at = PARTS + 3 * p + n
        return remote(wx_send.at[p, n], wx_recv.at[p, n], w_ss.at[at], w_rs.at[at], to)

    def w_level(p, m):
        to = (2 * (PARTS * m + p) + xh) * 2 + core
        return remote(wz_send.at[p, m], wz_recv.at[z], w_ss.at[4 * PARTS], w_rs.at[4 * PARTS], (to, f))

    def w_levels():
        every = wz_recv.at[pl.ds(0, levels - 1)]
        return remote(every, every, w_ss.at[4 * PARTS], w_rs.at[4 * PARTS], (mate, f))

    def w_pair_start(p):
        @pl.loop(0, levels_of_part)
        def _(m):
            for n in range(2):
                for x in range(2):
                    wp_send[p, n, x, m] = part[1 - core, n, x, p, m].astype(BF16)

        w_pair(p).start()

    def w_cross_start(p):
        w_pair(p).wait_recv()
        for n in (1, 0, 2):
            xh_there, xl_there = ring_x[n]

            @pl.loop(0, levels_of_part)
            def _(m):
                total = part[core, xh_there, xl_there, p, m]
                total = total + wp_recv[p, xh_there, xl_there, m].astype(F32)
                wx_send[p, n, m] = total.astype(BF16)

            w_cross(p, n).start()

    def w_level_start(p):
        for n in range(3):
            w_cross(p, n).wait_recv()

        @pl.loop(0, levels_of_part)
        def _(m):
            total = part[core, xh, xl, p, m] + wp_recv[p, xh, xl, m].astype(F32)
            for n in range(3):
                total = total + wx_recv[p, n, m].astype(F32)
            wz_send[p, m] = total.astype(BF16)

        @pl.when(z % PARTS == p)
        def _():
            wz_recv[z] = wz_send[p, z // PARTS]

        @pl.loop(0, levels_of_part)
        def _(j):
            m = (z // PARTS + j) % levels_of_part

            @pl.when(PARTS * m + p != z)
            def _():
                w_level(p, m).start()

    at_every().wait_recv()
    w_part(0)
    w_pair_start(0)
    for p in range(1, PARTS):
        w_part(p)
        w_pair_start(p)
        w_cross_start(p - 1)
    qg[1].run()
    qg[2].run()
    w_cross_start(PARTS - 1)
    qg[3].run()
    for n in range(4):
        local_pair(n)
    qg[0].finish()
    w_level_start(0)
    w_level_start(1)
    w_level_start(2)

    def final_pair(n):
        for column in pairs[n]:
            for u in range(2):
                h = 2 * column + u
                after = state[1, h]
                grad = dot(v_of(h), after, NT) + acc_k[:, head_cols(h)]
                kg_ref[:, head_cols(h)] = (factor * grad).astype(BF16)
                grad = dot(k_of(h), after) + acc_v[:, head_cols(h)]
                vg_ref[:, head_cols(h)] = (factor * grad).astype(BF16)

    for n in range(1, 3):
        qg[n].finish()
    w_level_start(3)
    for n in range(3):
        qg[n].wait()
        final_pair(n)
    qg[3].finish()
    qg[3].wait()
    final_pair(3)
    for copy in (*own, *past_up, *past_down):
        copy.wait_send()

    for n, row in enumerate((up, down, far)):
        g_copy(n, row).wait_send()
    w_side.wait_send()
    w_share.wait_send()
    at_every().wait_send()
    kv.drain()
    for scan in qg:
        scan.drain()
    for p in range(PARTS):
        w_pair(p).wait_send()
        for n in range(3):
            w_cross(p, n).wait_send()
    w_levels().wait_recv()
    total = wz_recv[0].astype(F32)
    for j in range(1, levels):
        total = total + wz_recv[j].astype(F32)
    wg_ref[...] = total * grad_factor
    w_levels().wait_send()


def store(*refs):
    sems = refs[-1]
    copies = [pltpu.make_async_copy(refs[i], refs[4 + i], sems.at[i]) for i in range(4)]
    for copy in copies:
        copy.start()
    for copy in copies:
        copy.wait()


def body(queries, key_vectors, value_vectors, out_grad, out_weight):
    seq_devices = lax.axis_size("seq")
    group = lax.axis_size("fsdp")
    chips = seq_devices // 2
    _, tokens, width_all = queries.shape
    depth, width = out_weight.shape
    factor = 1.0 / math.sqrt(HEAD_DIM * tokens * seq_devices)
    grad_factor = 1.0 / math.sqrt(group * tokens * seq_devices)
    half = HEADS // 2
    out_rows = depth // seq_devices
    flat = (tokens, width_all)
    vmem = pl.BlockSpec(memory_space=pltpu.VMEM)
    levels = chips // 2
    ring = group // 2
    pieces = (levels // PARTS, out_rows, width)
    blocks = pltpu.VMEM((group, tokens, width), BF16)
    square = (HEAD_DIM, HEAD_DIM)
    chunk = (4, 2)
    dma = pltpu.SemaphoreType.DMA
    shapes = (
        jax.ShapeDtypeStruct(flat, BF16),
        jax.ShapeDtypeStruct(flat, BF16),
        jax.ShapeDtypeStruct(flat, BF16),
        jax.ShapeDtypeStruct((out_rows, width), F32),
    )
    args = [x.reshape(flat) for x in (queries, key_vectors, value_vectors, out_grad)]
    args = [pltpu.with_memory_space_constraint(x, pltpu.HBM) for x in (*args, out_weight)]
    results = pl.pallas_call(
        functools.partial(kernel, chips, group // 2, factor, grad_factor),
        out_shape=shapes,
        in_specs=[pl.BlockSpec(memory_space=pltpu.HBM)] * 5,
        out_specs=(vmem,) * 4,
        scratch_shapes=[
            pltpu.VMEM(flat, BF16),
            pltpu.VMEM(flat, BF16),
            pltpu.VMEM(flat, BF16),
            pltpu.VMEM((2, depth, width), BF16),
            pltpu.VMEM((ring, tokens, depth), BF16),
            blocks,
            pltpu.VMEM((3, 2, tokens, width), BF16),
            pltpu.VMEM((ring, tokens, 2 * width), BF16),
            pltpu.VMEM((ring, tokens, 2 * width), BF16),
            pltpu.VMEM((half,) + square, F32),
            pltpu.VMEM((half,) + square, F32),
            pltpu.VMEM((half,) + square, F32),
            pltpu.VMEM((4, chips, half * HEAD_DIM // chips, HEAD_DIM), BF16),
            pltpu.VMEM((half,) + square, BF16),
            pltpu.VMEM(chunk + square, F32),
            pltpu.VMEM(chunk + square, F32),
            pltpu.VMEM(chunk + square, F32),
            pltpu.VMEM((4, 4, chips, 2 * HEAD_DIM // chips, HEAD_DIM), BF16),
            pltpu.VMEM(chunk + square, BF16),
            pltpu.VMEM((2, HEADS) + square, BF16),
            pltpu.VMEM(flat, F32),
            pltpu.VMEM(flat, F32),
            pltpu.VMEM(flat, F32),
            pltpu.VMEM((2, 2, 2, PARTS, levels // PARTS, out_rows, width), F32),
            pltpu.VMEM((PARTS, 2, 2) + pieces, BF16),
            pltpu.VMEM((PARTS, 2, 2) + pieces, BF16),
            pltpu.VMEM((PARTS, 3) + pieces, BF16),
            pltpu.VMEM((PARTS, 3) + pieces, BF16),
            pltpu.VMEM((PARTS,) + pieces, BF16),
            pltpu.VMEM((levels, out_rows, width), BF16),
            dma((5,)),
            dma((3, 4)),
            dma((ring, 4)),
            dma((3,)),
            dma((ring,)),
            dma((1,)),
            dma((1,)),
            dma((10,)),
            dma((10,)),
            dma((10,)),
            dma((10,)),
            dma((4 * PARTS + 3,)),
            dma((4 * PARTS + 3,)),
        ],
        compiler_params=pltpu.CompilerParams(
            collective_id=0, has_side_effects=True, vmem_limit_bytes=44 * 1024 * 1024
        ),
    )(*args)
    results = pl.pallas_call(
        store,
        out_shape=shapes,
        in_specs=[vmem] * 4,
        out_specs=(pl.BlockSpec(memory_space=pltpu.HBM),) * 4,
        scratch_shapes=[dma((4,))],
        compiler_params=pltpu.CompilerParams(vmem_limit_bytes=16 * 1024 * 1024),
    )(*results)
    whole = (1,) + flat
    return (
        results[0].reshape(whole),
        results[1].reshape(whole),
        results[2].reshape(whole),
        results[3],
    )


def solution(mesh):
    in_specs = (
        P("fsdp", "seq", None),
        P("fsdp", "seq", None),
        P("fsdp", "seq", None),
        P("fsdp", "seq", None),
        P(None, "fsdp"),
    )
    out_specs = (
        P("fsdp", "seq", None),
        P("fsdp", "seq", None),
        P("fsdp", "seq", None),
        P("seq", "fsdp"),
    )
    return jax.shard_map(body, mesh=mesh, in_specs=in_specs, out_specs=out_specs, check_vma=False)
```
